128 devices in a mesh: pool: 8 (over x, y_lo), expert: 16 (over y_hi, z, core).
Axes of the slice: x: 4, y: 4 (y_hi: 2, y_lo: 2; y = y_hi * 2 + y_lo), z: 4, core: 2. Of those that a mesh axis runs over, the one named last changes fastest.
Arguments:
- queries: bfloat16 [4096, 4096], P(('pool', 'expert')), may hold values from -6 to 6
- kv_cache: bfloat16 [4096, 64, 1024], P(('pool', 'expert')), may hold values from -6 to 6
- block_index: int32 [4096, 8], P(('pool', 'expert')), may hold values from 0 to 31, as said below
- lengths: int32 [4096], P(('pool', 'expert')), may hold values from 2 to 512, as said below
- residual: bfloat16 [4096, 2048], P('pool', 'expert'), may hold values from -21 to 21
- out_weight: bfloat16 [4096, 2048], P(None, 'expert'), may hold values from -0.09375 to 0.09375
- norm_gain: float32 [2048], P('expert'), may hold values from 0.25 to 1.75
- expert_ids: int32 [4096, 8], P('pool'), may hold values from 0 to 127, all different within a row; in each aligned block of 512 rows (0 to 511, 512 to 1023, ...) at most 64 rows name the same one
- route_weights: float32 [4096, 8], P('pool'), may hold values from 0.02 to 0.25
- gate_weight: bfloat16 [128, 2048, 768], P(('pool', 'expert')), may hold values from -0.125 to 0.125
- up_weight: bfloat16 [128, 2048, 768], P(('pool', 'expert')), may hold values from -0.125 to 0.125
- down_weight: bfloat16 [128, 768, 2048], P(('pool', 'expert')), may hold values from -0.21875 to 0.21875
Outputs:
- attended: bfloat16 [4096, 2048], P('pool', 'expert')
- expert_mix: bfloat16 [4096, 2048], P('pool', 'expert')
The draws below stay inside these ranges and needn't reach their ends.
Inputs may be any that keep to these rules, and one draw needn't show every extreme that they name: Sequence t reads blocks of the pool of 32 blocks held with it: block (t // 32) * 32 + block_index[t, j] of kv_cache. The first lengths[t] of the sequence's 8 * 64 positions are live. `expert_ids`: each row names 8 different experts; within the 512 rows of one index of pool no expert is named by more than 64 rows.
All inputs are finite; a program needn't handle non-finite values.
Results may differ from the reference program's by a relative error of at most 0.01.
Values may be sent and summed in bfloat16 or wider, within the bound.
A program may use at most 128 MiB of HBM per device.

```python
import math
import jax
import jax.numpy as jnp
import numpy as np
from jax import lax

D = 2048
HEADS = 32
KV_HEADS = 4
HEAD_DIM = 128
F = 768
TOPK = 8
BLOCK = 64
NBLK = 8
TOK_DEV = 32
BLOCKS_DEV = 32
EXPERTS = 128
TOKENS = 4096
GROUP_ROWS = 512
CAP = 64
BLOCKS = 4096
KVW = 1024
N_POOL = 8


def index_table(key):
    return jax.random.randint(jax.random.fold_in(key, 11), (TOKENS, NBLK), 0, BLOCKS_DEV).astype(jnp.int32)


def draw_block_index(key, part):
    return index_table(key)


def draw_lengths(key, part):
    drawn_lengths = jax.random.randint(jax.random.fold_in(key, 31), (TOKENS,), 2, NBLK * BLOCK + 1)
    row_ids = jnp.arange(TOKENS, dtype=jnp.int32)
    return jnp.where(row_ids % TOK_DEV == 0, NBLK * BLOCK, drawn_lengths).astype(jnp.int32)


def draw_queries(key, part):
    normal_part = jnp.clip(jax.random.normal(jax.random.fold_in(key, 41), (TOKENS, HEADS, HEAD_DIM), jnp.float32), -6.0, 6.0)
    return normal_part.reshape(TOKENS, HEADS * HEAD_DIM).astype(jnp.bfloat16)


def draw_kv_cache(key, part):
    normal_part = jnp.clip(jax.random.normal(jax.random.fold_in(key, 51), (BLOCKS, BLOCK, KVW), jnp.float32), -6.0, 6.0)
    return normal_part.astype(jnp.bfloat16)


def draw_residual(key, part):
    column_pos = jnp.arange(D, dtype=jnp.float32) / (D - 1)
    noise = jnp.clip(jax.random.normal(jax.random.fold_in(key, 64), (TOKENS, D), jnp.float32), -6.0, 6.0)
    return (noise * 0.5 * jnp.exp(math.log(3.0) * column_pos)[None, :]).astype(jnp.bfloat16)


def block_scale(key, shape, split, smallest, largest):
    gain, own = 1.0, jax.random.fold_in(key, 6)
    for axis_at, shards_of in split:
        heights = jnp.exp(jax.random.uniform(jax.random.fold_in(own, axis_at), (shards_of,), jnp.float32, smallest / len(split), largest / len(split)))
        gain = gain * jnp.repeat(heights, shape[axis_at] // shards_of).reshape([-1 if axis == axis_at else 1 for axis in range(len(shape))])
    return gain


def shared_out(stream_key, own, number, rows, number_of, top, most, skew):
    sequence = jax.random.permutation(stream_key, number_of)
    heavy_load, common = load_shares(number_of, rows * top, most, skew, True), load_shares(number_of, rows * top, most, skew, False)
    places = jnp.arange(number_of)

    def named(tallies, rotation):
        used = int((tallies > 0).sum())
        fixed = max(1, used // 4)
        shifted = fixed + (places - fixed + rotation * (used - fixed)) % max(1, number_of - fixed)
        return jnp.zeros((number_of,), jnp.int32).at[sequence[jnp.where(places < fixed, places, shifted)]].set(jnp.asarray(tallies, jnp.int32))

    tallies = jnp.where(number % 4 == 0, named(heavy_load, number // 4), named(common, number - number // 4 - 1))
    mixed = jax.random.permutation(jax.random.fold_in(own, 3), number_of)
    source_of, receiver = mixed[0:number_of // 2 * 2:2], mixed[1:number_of // 2 * 2:2]
    margin = jnp.minimum(tallies[source_of] - 1, most - tallies[receiver]) // 2
    margin = jnp.where((source_of == sequence[0]) | (receiver == sequence[0]) | (tallies[receiver] == 0), 0, jnp.maximum(margin, 0))
    shifted = jax.random.randint(jax.random.fold_in(own, 4), (number_of // 2,), 0, 1 << 20) % (margin + 1)
    tallies = tallies.at[source_of].add(-shifted).at[receiver].add(shifted)
    members = jnp.searchsorted(jnp.cumsum(tallies), jnp.arange(rows * top), side="right").astype(jnp.int32)
    grid = members.reshape(top, rows).T
    grid = grid[jax.random.permutation(jax.random.fold_in(own, 1), rows)]
    rotation = jax.random.randint(jax.random.fold_in(own, 2), (rows, 1), 0, top)
    return jnp.take_along_axis(grid, (jnp.arange(top)[None, :] + rotation) % top, axis=1)


def load_shares(number_of, total, limit, skew, full):
    loads = [(1 << 20) // math.isqrt(rank ** skew) + 1 for rank in range(1, number_of + 1)]
    largest = limit if full else min(limit, max(-(-total // number_of), total * loads[0] // sum(loads)))
    least = 1 if total - largest >= number_of - 1 else 0
    holding, surplus = [largest] + [least] * (number_of - 1), total - largest - least * (number_of - 1)
    while surplus > 0:
        free = [i for i in range(1, number_of) if holding[i] < largest] or [i for i in range(1, number_of) if holding[i] < limit]
        mass, budget = sum([loads[i] for i in free]), surplus
        for i in free:
            extra = min(limit - holding[i], max(1, budget * loads[i] // mass), surplus)
            holding[i] = holding[i] + extra
            surplus = surplus - extra
    return np.array(holding)


def gaussian(own_key, extent, width, limit, split=(), kind=jnp.bfloat16):
    drawn = width * jax.random.normal(own_key, extent, jnp.float32)
    if split:
        drawn = drawn * block_scale(own_key, extent, split, -0.22, 0.18)
    return jnp.clip(drawn, -limit, limit).astype(kind)


def setup_inputs(seed: int = 0) -> dict:
    streams_of = jax.random.split(jax.random.key(seed), 13)
    queries = draw_queries(jax.random.fold_in(streams_of[12], 71), 0)
    kv_cache = draw_kv_cache(jax.random.fold_in(streams_of[12], 71), 0)
    block_index = draw_block_index(jax.random.fold_in(streams_of[12], 71), 0)
    lengths = draw_lengths(jax.random.fold_in(streams_of[12], 71), 0)
    residual = draw_residual(jax.random.fold_in(streams_of[12], 71), 0)
    out_weight = gaussian(streams_of[5], (HEADS * HEAD_DIM, D), (HEADS * HEAD_DIM) ** -0.5, 0.09375, ((1, 16),))
    norm_gain = jnp.clip(1.0 + 0.15 * jax.random.normal(streams_of[6], (D,), jnp.float32), 0.25, 1.75)
    expert_ids_keys = jax.random.split(jax.random.fold_in(streams_of[7], 1), TOKENS // GROUP_ROWS)
    expert_ids_turns = jax.random.permutation(jax.random.fold_in(streams_of[7], 3), TOKENS // GROUP_ROWS)
    expert_ids = jax.vmap(lambda own, number: shared_out(jax.random.fold_in(streams_of[7], 2), own, number, GROUP_ROWS, EXPERTS, TOPK, CAP, 2))(expert_ids_keys, expert_ids_turns).reshape((TOKENS, TOPK))
    route_weights = jnp.clip(0.02 + 0.23 * jax.random.uniform(streams_of[8], (TOKENS, TOPK), jnp.float32) ** block_scale(streams_of[8], (TOKENS, TOPK), ((0, 8),), -0.2, 0.2), 0.02, 0.25)
    gate_weight = gaussian(streams_of[9], (EXPERTS, D, F), D ** -0.5, 0.125, ((0, 128),))
    up_weight = gaussian(streams_of[10], (EXPERTS, D, F), D ** -0.5, 0.125, ((0, 128),))
    down_weight = gaussian(streams_of[11], (EXPERTS, F, D), F ** -0.5, 0.21875, ((0, 128),))
    return dict(queries=queries, kv_cache=kv_cache, block_index=block_index, lengths=lengths, residual=residual, out_weight=out_weight, norm_gain=norm_gain, expert_ids=expert_ids, route_weights=route_weights, gate_weight=gate_weight, up_weight=up_weight, down_weight=down_weight)


epsilon = 1e-06

def attend_rows(queries, kv_cache, block_index, lengths):
    context = NBLK * BLOCK
    half_width = KV_HEADS * HEAD_DIM
    group_size = HEADS // KV_HEADS
    owners = jnp.arange(TOKENS, dtype=jnp.int32) // TOK_DEV * BLOCKS_DEV
    global_blocks = (block_index + owners[:, None]).astype(jnp.int32)
    positions = jnp.arange(context, dtype=jnp.int32)

    def one_row(inputs):
        query_row, blocks_row, length_row = inputs
        gathered = kv_cache[blocks_row].reshape(context, 2 * half_width)
        key_part = gathered[:, :half_width].reshape(context, KV_HEADS, HEAD_DIM).astype(jnp.float32)
        value_part = gathered[:, half_width:].reshape(context, KV_HEADS, HEAD_DIM).astype(jnp.float32)
        query_split = query_row.reshape(KV_HEADS, group_size, HEAD_DIM).astype(jnp.float32)
        scores = jnp.einsum('gqd,pgd->gqp', query_split, key_part) * HEAD_DIM ** (-0.5)
        live_mask = positions < length_row
        scores = jnp.where(live_mask[None, None, :], scores, -1e+30)
        maximum = lax.optimization_barrier(jnp.max(scores, axis=-1, keepdims=True))
        exponent = jnp.exp(scores - maximum)
        softmax_w = (exponent / lax.optimization_barrier(jnp.sum(exponent, axis=-1, keepdims=True))).astype(jnp.bfloat16)
        attended_part = jnp.einsum('gqp,pgd->gqd', softmax_w.astype(jnp.float32), value_part)
        return attended_part.astype(jnp.bfloat16).reshape(HEADS * HEAD_DIM)
    return lax.map(one_row, (queries, global_blocks, lengths))

def expert_ffn(inputs):
    rows_in, gate_w, up_w, down_w = inputs
    gate_act = jnp.dot(rows_in, gate_w, preferred_element_type=jnp.float32)
    upper = jnp.dot(rows_in, up_w, preferred_element_type=jnp.float32)
    hidden = (jax.nn.silu(gate_act) * upper).astype(jnp.bfloat16)
    return jnp.dot(hidden, down_w, preferred_element_type=jnp.float32).astype(jnp.bfloat16)

def reference(queries, kv_cache, block_index, lengths, residual, out_weight, norm_gain, expert_ids, route_weights, gate_weight, up_weight, down_weight):
    attention = attend_rows(queries, kv_cache, block_index, lengths)
    projected = jnp.dot(attention, out_weight, preferred_element_type=jnp.float32)
    attended = (residual.astype(jnp.float32) + projected).astype(jnp.bfloat16)
    attended_f = attended.astype(jnp.float32)
    square_sum = lax.optimization_barrier(jnp.sum(attended_f * attended_f, axis=1, keepdims=True))
    normed = (attended_f * lax.rsqrt(square_sum / D + epsilon) * norm_gain[None, :]).astype(jnp.bfloat16)
    flat_ids = expert_ids.reshape(N_POOL, GROUP_ROWS * TOPK)
    onehot = (flat_ids[:, :, None] == jnp.arange(EXPERTS, dtype=jnp.int32)[None, None, :]).astype(jnp.int32)
    before = jnp.cumsum(onehot, axis=1) - onehot
    slot_ids = lax.optimization_barrier(jnp.sum(before * onehot, axis=2)).astype(jnp.int32)
    row_place = (jnp.arange(N_POOL, dtype=jnp.int32)[:, None] * CAP + slot_ids).reshape(-1)
    expert_flat = flat_ids.reshape(-1)
    sources = jnp.repeat(normed, TOPK, axis=0)
    buffers = jnp.zeros((EXPERTS, N_POOL * CAP, D), jnp.bfloat16).at[expert_flat, row_place].set(sources)
    expert_out = lax.map(expert_ffn, (buffers, gate_weight, up_weight, down_weight))
    picked = expert_out[expert_flat, row_place].reshape(TOKENS, TOPK, D).astype(jnp.float32)
    expert_mix = lax.optimization_barrier(jnp.sum(picked * route_weights[:, :, None], axis=1)).astype(jnp.bfloat16)
    return (attended, expert_mix)
```

```python
import math

import jax
import jax.numpy as jnp
from jax import lax
from jax.experimental import pallas as pl
from jax.experimental.pallas import tpu as pltpu
from jax.sharding import PartitionSpec as P

HD = 128
EPS = 1e-06
MESH = pl.DeviceIdType.MESH
F32 = jnp.float32
BF16 = jnp.bfloat16
VM = pl.BlockSpec(memory_space=pltpu.VMEM)
ANY = pl.BlockSpec(memory_space=pl.ANY)
NT = (((1,), (1,)), ((), ()))
TN = (((0,), (0,)), ((), ()))


def attend_project(
    q_ref,
    kv_hbm,
    bi_ref,
    len_ref,
    res_ref,
    w_hbm,
    gain_ref,
    att_ref,
    gall_ref,
    kv,
    wown,
    wsib,
    ressib,
    gath,
    s_scr,
    p_scr,
    linv,
    bias,
    stage,
    acc,
    in_sem,
    w_sem,
    y_s,
    y_r,
    z_s,
    z_r,
    sib_s,
    sib_r,
    gain_s,
    gain_r,
):
    e = lax.axis_index("expert")
    core = e % 2
    chip = e // 2
    y_hi = chip // 4
    z = chip % 4
    sib = e + 1 - 2 * core
    chip_y = chip + 4 - 8 * y_hi
    z_up = (z + 1) % 4
    z_dn = (z + 3) % 4
    z_op = (z + 2) % 4
    chip_up = y_hi * 4 + z_up
    chip_dn = y_hi * 4 + z_dn
    chip_op = y_hi * 4 + z_op
    flip = 4 - 8 * y_hi
    dev_y = chip_y * 2 + core
    dev_up = chip_up * 2 + core
    dev_dn = chip_dn * 2 + core

    barrier = pltpu.get_barrier_semaphore()
    for d in range(1, 16):
        pl.semaphore_signal(barrier, inc=1, device_id={"expert": (e + d) % 16}, device_id_type=MESH)

    def fetch(i):
        return pltpu.make_async_copy(kv_hbm.at[:, pl.ds(i * HD, HD)], kv.at[i], in_sem.at[i])

    fetch_w = pltpu.make_async_copy(w_hbm, wown, w_sem)
    for g in range(4):
        fetch(g).start()
        fetch(4 + g).start()
    fetch_w.start()

    rows, span = bias.shape
    lane = lax.broadcasted_iota(jnp.int32, (rows, span), 1)
    block = lane // 64
    offset = lane % 64
    count = jnp.zeros((rows, span), F32)
    for j in range(8):
        live = (block == bi_ref[:, j : j + 1]) & (offset < len_ref[...] - 64 * j)
        count = count + jnp.where(live, 1.0, 0.0)
    bias[...] = jnp.where(count > 0.0, jnp.log2(jnp.maximum(count, 1.0)), -1e30)

    factor = HD ** (-0.5) * math.log2(math.e)

    def attend(g):
        fetch(g).wait()
        query = jnp.concatenate(
            [q_ref[:, (g * 8 + i) * HD : (g * 8 + i + 1) * HD] for i in range(8)], axis=0
        )
        s_scr[...] = lax.dot_general(query, kv[g], NT, preferred_element_type=F32)

        def soften(r, carry):
            at = pl.ds(pl.multiple_of(r * 16, 16), 16)
            of = pl.ds(pl.multiple_of((r % 2) * 16, 16), 16)
            x = s_scr[at, :] * factor + bias[of, :]
            top = jnp.max(x, axis=1, keepdims=True)
            ex = jnp.exp2(x - top)
            total = jnp.sum(ex, axis=1, keepdims=True)
            p_scr[at, :] = ex.astype(BF16)
            linv[at, :] = jnp.broadcast_to(1.0 / total, (16, HD))
            return carry

        lax.fori_loop(0, 16, soften, 0)
        fetch(4 + g).wait()
        o = jnp.dot(p_scr[...], kv[4 + g], preferred_element_type=F32) * linv[...]
        o = o.astype(BF16)
        for i in range(8):
            gath[chip, g, :, i * HD : (i + 1) * HD] = o[i * 32 : (i + 1) * 32]

    def remote(src, dst, ssem, rsem, dev):
        return pltpu.make_async_remote_copy(
            src_ref=src,
            dst_ref=dst,
            send_sem=ssem,
            recv_sem=rsem,
            device_id={"expert": dev},
            device_id_type=MESH,
        )

    lo, hi = pl.ds(0, 16), pl.ds(16, 16)

    def block_copy(c, g, ssem, rsem, dev, part=None):
        ref = gath.at[c, g] if part is None else gath.at[c, g, part]
        return remote(ref, ref, ssem, rsem, dev)

    def own_y(g):
        return block_copy(chip, g, y_s.at[g], y_r.at[g], dev_y)

    def z_copy(kind, g, way):
        dev = dev_up if way == 0 else dev_dn
        ss, rs = z_s.at[kind, g, way], z_r.at[kind, g, way]
        if kind == 0:
            return block_copy(chip, g, ss, rs, dev)
        if kind == 1:
            return block_copy(chip_y, g, ss, rs, dev)
        source = chip_dn if way == 0 else chip_up
        if kind == 3:
            source = source + flip
        return block_copy(source, g, ss, rs, dev, lo if way == 0 else hi)

    def send_own(g):
        z_copy(0, g, 0).start()
        z_copy(0, g, 1).start()
        own_y(g).start()

    def send_partner(g):
        own_y(g).wait_recv()
        z_copy(1, g, 0).start()
        z_copy(1, g, 1).start()

    def relay(kind, g):
        for way in (0, 1):
            z_copy(kind, g, way).wait_recv()
            z_copy(kind + 2, g, way).start()

    def finish(g):
        for way in (0, 1):
            z_copy(2, g, way).wait_recv()
            z_copy(3, g, way).wait_recv()

    def project(g):
        depth = 8 * HD
        at = pl.ds(g * depth, depth)
        rows_g = gath[:, g].reshape(256, depth)
        part = jnp.dot(rows_g, wown[at, :], preferred_element_type=F32)
        other = jnp.dot(rows_g, wsib[at, :], preferred_element_type=F32)
        if g == 0:
            acc[0] = part
            acc[1] = other
        else:
            acc[0] += part
            acc[1] += other

    attend(0)
    pl.semaphore_wait(barrier, 15)
    send_own(0)
    send_w = remote(w_hbm, wsib, sib_s.at[0], sib_r.at[0], sib)
    send_w.start()
    send_res = remote(res_ref.at[:, 1 - core], ressib, sib_s.at[1], sib_r.at[1], sib)
    send_res.start()
    gall_ref[e] = gain_ref[...]
    gains = [
        remote(gain_ref, gall_ref.at[e], gain_s.at[d], gain_r.at[d], (e + d) % 16)
        for d in range(1, 16)
    ]
    for gain in gains:
        gain.start()
    attend(1)
    send_own(1)
    send_partner(0)
    relay(0, 0)
    attend(2)
    send_own(2)
    relay(1, 0)
    send_partner(1)
    relay(0, 1)
    attend(3)
    send_own(3)
    relay(1, 1)
    send_partner(2)
    relay(0, 2)
    fetch_w.wait()
    send_w.wait_recv()
    finish(0)
    project(0)
    relay(1, 2)
    send_partner(3)
    relay(0, 3)
    finish(1)
    project(1)
    relay(1, 3)
    finish(2)
    project(2)
    finish(3)
    project(3)
    send_res.wait_recv()
    stage[...] = (ressib[...].astype(F32) + acc[1].reshape(8, 32, HD)).astype(BF16)
    send_out = remote(stage, att_ref.at[:, core], sib_s.at[2], sib_r.at[2], sib)
    send_out.start()
    att_ref[:, core] = (res_ref[:, core].astype(F32) + acc[0].reshape(8, 32, HD)).astype(BF16)
    for g in range(4):
        own_y(g).wait_send()
        for kind in range(4):
            z_copy(kind, g, 0).wait_send()
            z_copy(kind, g, 1).wait_send()
    send_w.wait_send()
    send_res.wait_send()
    for gain in gains:
        gain.wait()
    send_out.wait()


def attention_stage(queries, kv_cache, block_index, lengths, residual, out_weight, norm_gain):
    rows = queries.shape[0]
    span = kv_cache.shape[0] * kv_cache.shape[1]
    width = kv_cache.shape[2]
    dma = pltpu.SemaphoreType.DMA
    att, gall = pl.pallas_call(
        attend_project,
        out_shape=(
            jax.ShapeDtypeStruct((8, 2, 32, HD), BF16),
            jax.ShapeDtypeStruct((16, 1, HD), F32),
        ),
        in_specs=[VM, ANY, VM, VM, VM, ANY, VM],
        out_specs=(VM, VM),
        scratch_shapes=[
            pltpu.VMEM((width // HD, span, HD), BF16),
            pltpu.VMEM(out_weight.shape, BF16),
            pltpu.VMEM(out_weight.shape, BF16),
            pltpu.VMEM((8, 32, HD), BF16),
            pltpu.VMEM((8, 4, 32, 8 * HD), BF16),
            pltpu.VMEM((256, span), F32),
            pltpu.VMEM((256, span), BF16),
            pltpu.VMEM((256, HD), F32),
            pltpu.VMEM((rows, span), F32),
            pltpu.VMEM((8, 32, HD), BF16),
            pltpu.VMEM((2, 256, HD), F32),
            dma((8,)),
            dma,
            dma((4,)),
            dma((4,)),
            dma((4, 4, 2)),
            dma((4, 4, 2)),
            dma((3,)),
            dma((3,)),
            dma((16,)),
            dma((16,)),
        ],
        compiler_params=pltpu.CompilerParams(
            collective_id=0, has_side_effects=True, vmem_limit_bytes=60 * 1024 * 1024
        ),
        name="attend_project",
    )(
        queries,
        kv_cache.reshape(span, width),
        block_index,
        lengths.reshape(rows, 1),
        residual.reshape(8, 2, 32, HD),
        out_weight,
        norm_gain.reshape(1, HD),
    )
    return att.reshape(512, HD), gall.reshape(1, 16 * HD)


def dispatch(ids_ref, rw_ref, x_ref, out_ref, slot_ref, wt_ref):
    experts, rows = slot_ref.shape
    which = lax.broadcasted_iota(jnp.int32, (experts, rows), 0)
    named = jnp.zeros((experts, rows), F32)
    weight = jnp.zeros((experts, rows), F32)
    for k in range(8):
        same = which == ids_ref[k : k + 1, :]
        named = named + jnp.where(same, 1.0, 0.0)
        weight = weight + jnp.where(same, rw_ref[k : k + 1, :], 0.0)
    wt_ref[...] = weight
    early = lax.broadcasted_iota(jnp.int32, (rows, rows), 0)
    late = lax.broadcasted_iota(jnp.int32, (rows, rows), 1)
    ahead = jnp.where(early < late, 1.0, 0.0).astype(BF16)
    slot = jnp.dot(named.astype(BF16), ahead, preferred_element_type=F32)
    slot_ref[...] = jnp.where(named > 0.0, slot, -1.0)
    place = lax.broadcasted_iota(jnp.int32, (64, rows), 0).astype(F32)

    def some(i, carry):
        parts = [
            jnp.where(slot_ref[pl.ds(i * 4 + u, 1), :] == place, 1.0, 0.0).astype(BF16)
            for u in range(4)
        ]
        chosen = jnp.concatenate(parts, axis=0)
        out_ref[pl.ds(pl.multiple_of(i * 256, 256), 256), :] = jnp.dot(
            chosen, x_ref[...], preferred_element_type=F32
        ).astype(BF16)
        return carry

    lax.fori_loop(0, experts // 4, some, 0)


def expert_rows(x_ref, gain_ref, g_hbm, u_hbm, d_hbm, y_ref, gw, uw, dw, xs, hid, sem):
    copies = [
        pltpu.make_async_copy(g_hbm.at[0], gw, sem.at[0]),
        pltpu.make_async_copy(u_hbm.at[0], uw, sem.at[1]),
        pltpu.make_async_copy(d_hbm.at[0], dw, sem.at[2]),
    ]
    for copy in copies:
        copy.start()

    def norm(i, carry):
        p = i // 4
        at = pl.ds(pl.multiple_of((i % 4) * 16, 16), 16)
        x = jnp.concatenate([x_ref[p, f, at, :] for f in range(16)], axis=1).astype(F32)
        inv = lax.rsqrt(jnp.sum(x * x, axis=1, keepdims=True) / (16 * HD) + EPS)
        xs[pl.ds(pl.multiple_of(i * 16, 16), 16), :] = (x * inv * gain_ref[...]).astype(BF16)
        return carry

    lax.fori_loop(0, 32, norm, 0)
    copies[0].wait()
    copies[1].wait()

    def up(i, carry):
        at = pl.ds(pl.multiple_of(i * 256, 256), 256)
        gate = jnp.dot(xs[...], gw[:, at], preferred_element_type=F32)
        upper = jnp.dot(xs[...], uw[:, at], preferred_element_type=F32)
        hid[:, at] = (gate / (1.0 + jnp.exp(-gate)) * upper).astype(BF16)
        return carry

    lax.fori_loop(0, 3, up, 0)
    copies[2].wait()

    def down(i, carry):
        at = pl.ds(pl.multiple_of(i * 256, 256), 256)
        y = jnp.dot(hid[...], dw[:, at], preferred_element_type=F32).astype(BF16)
        for p in range(8):
            for h in range(2):
                y_ref[p, i * 2 + h] = y[p * 64 : (p + 1) * 64, h * HD : (h + 1) * HD]
        return carry

    lax.fori_loop(0, 8, down, 0)


def combine(slot_ref, wt_ref, y_ref, out_ref, acc):
    experts, rows = slot_ref.shape
    place = lax.broadcasted_iota(jnp.int32, (64, rows), 0).astype(F32)
    acc[...] = jnp.zeros_like(acc)

    def some(i, carry):
        parts = [
            jnp.where(
                slot_ref[pl.ds(i * 4 + u, 1), :] == place, wt_ref[pl.ds(i * 4 + u, 1), :], 0.0
            ).astype(BF16)
            for u in range(4)
        ]
        chosen = jnp.concatenate(parts, axis=0)
        y = y_ref[pl.ds(pl.multiple_of(i * 256, 256), 256), :]
        acc[...] += lax.dot_general(y, chosen, TN, preferred_element_type=F32)
        return carry

    lax.fori_loop(0, experts // 4, some, 0)
    out_ref[...] = acc[...].T.astype(BF16)


def shards(
    queries,
    kv_cache,
    block_index,
    lengths,
    residual,
    out_weight,
    norm_gain,
    expert_ids,
    route_weights,
    gate_weight,
    up_weight,
    down_weight,
):
    attended, gain = attention_stage(
        queries, kv_cache, block_index, lengths, residual, out_weight, norm_gain
    )
    big = pltpu.CompilerParams(vmem_limit_bytes=56 * 1024 * 1024)
    outgoing, slot, wt = pl.pallas_call(
        dispatch,
        out_shape=(
            jax.ShapeDtypeStruct((128 * 64, HD), BF16),
            jax.ShapeDtypeStruct((128, 512), F32),
            jax.ShapeDtypeStruct((128, 512), F32),
        ),
        in_specs=[VM] * 3,
        out_specs=(VM, VM, VM),
        compiler_params=big,
        name="dispatch",
    )(expert_ids.T, route_weights.T, attended)
    axes = ("pool", "expert")
    received = lax.all_to_all(outgoing.reshape(128, 64, HD), axes, 0, 0, tiled=True)
    width, hidden = gate_weight.shape[1:]
    result = pl.pallas_call(
        expert_rows,
        out_shape=jax.ShapeDtypeStruct((8, 16, 64, HD), BF16),
        in_specs=[VM, VM, ANY, ANY, ANY],
        out_specs=VM,
        scratch_shapes=[
            pltpu.VMEM((width, hidden), BF16),
            pltpu.VMEM((width, hidden), BF16),
            pltpu.VMEM((hidden, width), BF16),
            pltpu.VMEM((512, width), BF16),
            pltpu.VMEM((512, hidden), BF16),
            pltpu.SemaphoreType.DMA((3,)),
        ],
        compiler_params=big,
        name="expert_rows",
    )(received.reshape(8, 16, 64, HD), gain, gate_weight, up_weight, down_weight)
    returned = lax.all_to_all(result.reshape(128, 64, HD), axes, 0, 0, tiled=True)
    mixed = pl.pallas_call(
        combine,
        out_shape=jax.ShapeDtypeStruct((512, HD), BF16),
        in_specs=[VM] * 3,
        out_specs=VM,
        scratch_shapes=[pltpu.VMEM((HD, 512), F32)],
        compiler_params=big,
        name="combine",
    )(slot, wt, returned.reshape(128 * 64, HD))
    return (attended, mixed)


def solution(mesh):
    return jax.shard_map(
        shards,
        mesh=mesh,
        in_specs=(
            P(("pool", "expert"), None),
            P(("pool", "expert"), None, None),
            P(("pool", "expert"), None),
            P(("pool", "expert")),
            P("pool", "expert"),
            P(None, "expert"),
            P("expert"),
            P("pool", None),
            P("pool", None),
            P(("pool", "expert"), None, None),
            P(("pool", "expert"), None, None),
            P(("pool", "expert"), None, None),
        ),
        out_specs=(P("pool", "expert"), P("pool", "expert")),
        check_vma=False,
    )
```

```python
import math

import jax
import jax.numpy as jnp
from jax import lax
from jax.experimental import pallas as pl
from jax.experimental.pallas import tpu as pltpu
from jax.sharding import PartitionSpec as P

HD = 128
EPS = 1e-06
MESH = pl.DeviceIdType.MESH
F32 = jnp.float32
BF16 = jnp.bfloat16
VM = pl.BlockSpec(memory_space=pltpu.VMEM)
ANY = pl.BlockSpec(memory_space=pl.ANY)
NT = (((1,), (1,)), ((), ()))
TN = (((0,), (0,)), ((), ()))
SLOTS = 64


def layer(
    q_ref,
    kv_hbm,
    bi_ref,
    len_ref,
    res_ref,
    w_hbm,
    gain_ref,
    ids_ref,
    rw_ref,
    g_hbm,
    u_hbm,
    d_hbm,
    att_ref,
    mix_ref,
    kv,
    wown,
    wsib,
    ressib,
    gath,
    s_scr,
    p_scr,
    linv,
    bias,
    stage,
    acc,
    table,
    gall_ref,
    slot_ref,
    wt_ref,
    gw,
    uw,
    dw,
    obuf,
    rbuf,
    ybuf,
    zbuf,
    xs,
    hid,
    mixt,
    in_sem,
    w_sem,
    y_s,
    y_r,
    z_s,
    z_r,
    sib_s,
    sib_r,
    gain_s,
    gain_r,
    ffn_sem,
    out_s,
    out_r,
    back_s,
    back_r,
):
    p = lax.axis_index("pool")
    e = lax.axis_index("expert")
    core = e % 2
    chip = e // 2
    y_hi = chip // 4
    z = chip % 4
    sib = e + 1 - 2 * core
    chip_y = chip + 4 - 8 * y_hi
    z_up = (z + 1) % 4
    z_dn = (z + 3) % 4
    z_op = (z + 2) % 4
    chip_up = y_hi * 4 + z_up
    chip_dn = y_hi * 4 + z_dn
    chip_op = y_hi * 4 + z_op
    flip = 4 - 8 * y_hi
    dev_y = chip_y * 2 + core
    dev_up = chip_up * 2 + core
    dev_dn = chip_dn * 2 + core

    me = p * 16 + e
    barrier = pltpu.get_barrier_semaphore()

    def fetch(i):
        return pltpu.make_async_copy(kv_hbm.at[:, pl.ds(i * HD, HD)], kv.at[i], in_sem.at[i])

    fetch_w = pltpu.make_async_copy(w_hbm, wown, w_sem)
    for g in range(4):
        fetch(g).start()
        fetch(4 + g).start()
    fetch_w.start()
    ffn = [
        pltpu.make_async_copy(g_hbm.at[0], gw, ffn_sem.at[0]),
        pltpu.make_async_copy(u_hbm.at[0], uw, ffn_sem.at[1]),
        pltpu.make_async_copy(d_hbm.at[0], dw, ffn_sem.at[2]),
    ]
    for copy in ffn:
        copy.start()

    def greet(d, carry):
        t = lax.rem(me + d, 128)
        pl.semaphore_signal(
            barrier,
            inc=1,
            device_id={"pool": lax.div(t, 16), "expert": lax.rem(t, 16)},
            device_id_type=MESH,
        )
        return carry

    lax.fori_loop(1, 128, greet, 0)

    rows, span = bias.shape
    lane = lax.broadcasted_iota(jnp.int32, (rows, span), 1)
    block = lane // 64
    offset = lane % 64
    count = jnp.zeros((rows, span), F32)
    table[...] = jnp.zeros_like(table)
    table[0:8, 0:rows] = bi_ref[...]
    table[8:16, 0:rows] = jnp.broadcast_to(len_ref[...], (8, rows))
    turned = table[...].T[0:rows, :]
    for j in range(8):
        live = (block == turned[:, j : j + 1]) & (offset < turned[:, 8:9] - 64 * j)
        count = count + jnp.where(live, 1.0, 0.0)
    bias[...] = jnp.where(count > 0.0, jnp.log2(jnp.maximum(count, 1.0)), -1e30)

    factor = HD ** (-0.5) * math.log2(math.e)

    def attend(g):
        fetch(g).wait()
        query = jnp.concatenate(
            [q_ref[:, (g * 8 + i) * HD : (g * 8 + i + 1) * HD] for i in range(8)], axis=0
        )
        s_scr[...] = lax.dot_general(query, kv[g], NT, preferred_element_type=F32)

        def soften(r, carry):
            at = pl.ds(pl.multiple_of(r * 16, 16), 16)
            of = pl.ds(pl.multiple_of((r % 2) * 16, 16), 16)
            x = s_scr[at, :] * factor + bias[of, :]
            top = jnp.max(x, axis=1, keepdims=True)
            ex = jnp.exp2(x - top)
            total = jnp.sum(ex, axis=1, keepdims=True)
            p_scr[at, :] = ex.astype(BF16)
            linv[at, :] = jnp.broadcast_to(1.0 / total, (16, HD))
            return carry

        lax.fori_loop(0, 16, soften, 0)
        fetch(4 + g).wait()
        o = jnp.dot(p_scr[...], kv[4 + g], preferred_element_type=F32) * linv[...]
        o = o.astype(BF16)
        for i in range(8):
            gath[chip, g, :, i * HD : (i + 1) * HD] = o[i * 32 : (i + 1) * 32]

    def remote(src, dst, ssem, rsem, dev):
        return pltpu.make_async_remote_copy(
            src_ref=src,
            dst_ref=dst,
            send_sem=ssem,
            recv_sem=rsem,
            device_id={"expert": dev},
            device_id_type=MESH,
        )

    lo, hi = pl.ds(0, 16), pl.ds(16, 16)

    def block_copy(c, g, ssem, rsem, dev, part=None):
        ref = gath.at[c, g] if part is None else gath.at[c, g, part]
        return remote(ref, ref, ssem, rsem, dev)

    def own_y(g):
        return block_copy(chip, g, y_s.at[g], y_r.at[g], dev_y)

    def z_copy(kind, g, way):
        dev = dev_up if way == 0 else dev_dn
        ss, rs = z_s.at[kind, g, way], z_r.at[kind, g, way]
        if kind == 0:
            return block_copy(chip, g, ss, rs, dev)
        if kind == 1:
            return block_copy(chip_y, g, ss, rs, dev)
        source = chip_dn if way == 0 else chip_up
        if kind == 3:
            source = source + flip
        return block_copy(source, g, ss, rs, dev, lo if way == 0 else hi)

    def send_own(g):
        z_copy(0, g, 0).start()
        z_copy(0, g, 1).start()
        own_y(g).start()

    def send_partner(g):
        own_y(g).wait_recv()
        z_copy(1, g, 0).start()
        z_copy(1, g, 1).start()

    def relay(kind, g):
        for way in (0, 1):
            z_copy(kind, g, way).wait_recv()
            z_copy(kind + 2, g, way).start()

    def finish(g):
        for way in (0, 1):
            z_copy(2, g, way).wait_recv()
            z_copy(3, g, way).wait_recv()

    def project(g):
        depth = 8 * HD
        at = pl.ds(g * depth, depth)
        rows_g = gath[:, g].reshape(256, depth)
        part = jnp.dot(rows_g, wown[at, :], preferred_element_type=F32)
        other = jnp.dot(rows_g, wsib[at, :], preferred_element_type=F32)
        if g == 0:
            acc[0] = part
            acc[1] = other
        else:
            acc[0] += part
            acc[1] += other

    attend(0)
    pl.semaphore_wait(barrier, 127)
    send_own(0)
    send_w = remote(w_hbm, wsib, sib_s.at[0], sib_r.at[0], sib)
    send_w.start()
    send_res = remote(res_ref.at[:, 1 - core], ressib, sib_s.at[1], sib_r.at[1], sib)
    send_res.start()
    gall_ref[e] = gain_ref[...]
    gains = [
        remote(gain_ref, gall_ref.at[e], gain_s.at[d], gain_r.at[d], (e + d) % 16)
        for d in range(1, 16)
    ]
    for gain in gains:
        gain.start()
    attend(1)
    send_own(1)
    send_partner(0)
    relay(0, 0)
    attend(2)
    send_own(2)
    relay(1, 0)
    send_partner(1)
    relay(0, 1)
    attend(3)
    send_own(3)
    relay(1, 1)
    send_partner(2)
    relay(0, 2)
    experts, seqs = slot_ref.shape
    which = lax.broadcasted_iota(jnp.int32, (experts, seqs), 0)
    named = jnp.zeros((experts, seqs), F32)
    weight = jnp.zeros((experts, seqs), F32)
    for k in range(8):
        same = which == ids_ref[k : k + 1, :]
        named = named + jnp.where(same, 1.0, 0.0)
        weight = weight + jnp.where(same, rw_ref[k : k + 1, :], 0.0)
    wt_ref[...] = weight
    early = lax.broadcasted_iota(jnp.int32, (seqs, seqs), 0)
    late = lax.broadcasted_iota(jnp.int32, (seqs, seqs), 1)
    ahead = jnp.where(early < late, 1.0, 0.0).astype(BF16)
    slots = jnp.dot(named.astype(BF16), ahead, preferred_element_type=F32)
    slot_ref[...] = jnp.where(named > 0.0, slots, -1.0)
    fetch_w.wait()
    send_w.wait_recv()
    finish(0)
    project(0)
    relay(1, 2)
    send_partner(3)
    relay(0, 3)
    finish(1)
    project(1)
    relay(1, 3)
    finish(2)
    project(2)
    finish(3)
    project(3)
    send_res.wait_recv()
    stage[...] = (ressib[...].astype(F32) + acc[1].reshape(8, 32, HD)).astype(BF16)
    send_out = remote(stage, att_ref.at[:, core], sib_s.at[2], sib_r.at[2], sib)
    send_out.start()
    att_ref[:, core] = (res_ref[:, core].astype(F32) + acc[0].reshape(8, 32, HD)).astype(BF16)
    send_out.wait_recv()

    place = lax.broadcasted_iota(jnp.int32, (SLOTS, seqs), 0).astype(F32)
    px, py = p // 2, p % 2

    def target(d):
        d = lax.rem(d * 37, 128)
        c = lax.rem(core + d, 2)
        d = lax.div(d, 2)
        zz = lax.rem(z + d, 4)
        d = lax.div(d, 4)
        yh = lax.rem(y_hi + d, 2)
        d = lax.div(d, 2)
        yl = lax.rem(py + d, 2)
        d = lax.div(d, 2)
        xx = lax.rem(px + d, 4)
        return xx * 2 + yl, yh * 8 + zz * 2 + c

    def out_copy(d):
        tp, te = target(d)
        return pltpu.make_async_remote_copy(
            src_ref=obuf.at[tp * 16 + te],
            dst_ref=rbuf.at[me],
            send_sem=out_s,
            recv_sem=out_r,
            device_id={"pool": tp, "expert": te},
            device_id_type=MESH,
        )

    def pick(i):
        places, parts = [], []
        for u in range(4):
            tp, te = target(i * 4 + u)
            t = tp * 16 + te
            places.append(t)
            parts.append(jnp.where(slot_ref[pl.ds(t, 1), :] == place, 1.0, 0.0).astype(BF16))
        chosen = jnp.concatenate(parts, axis=0)
        picked = jnp.dot(chosen, att_ref[...].reshape(seqs, HD), preferred_element_type=F32)
        return places, picked.astype(BF16)

    places, picked = pick(0)
    rbuf[me] = picked[0:SLOTS]
    for u in range(1, 4):
        obuf[places[u]] = picked[u * SLOTS : (u + 1) * SLOTS]

    def some(i, carry):
        places, picked = pick(i)
        for u in range(4):
            obuf[places[u]] = picked[u * SLOTS : (u + 1) * SLOTS]
        for u in range(4):
            out_copy(i * 4 + u - 3).start()
        return carry

    lax.fori_loop(1, 32, some, 0)
    for u in range(3):
        out_copy(125 + u).start()

    everyone = pl.ds(0, 127)
    out_all = pltpu.make_async_remote_copy(
        src_ref=obuf.at[everyone],
        dst_ref=rbuf.at[everyone],
        send_sem=out_s,
        recv_sem=out_r,
        device_id={"pool": p, "expert": sib},
        device_id_type=MESH,
    )
    for gain in gains:
        gain.wait()
    gain_row = jnp.concatenate([gall_ref[f] for f in range(16)], axis=1)
    out_all.wait_recv()

    def norm(i, carry):
        at = pl.ds(pl.multiple_of(lax.rem(i, 4) * 16, 16), 16)
        first = lax.div(i, 4) * 16
        x = jnp.concatenate([rbuf[first + f, at, :] for f in range(16)], axis=1).astype(F32)
        inv = lax.rsqrt(jnp.sum(x * x, axis=1, keepdims=True) / (16 * HD) + EPS)
        xs[pl.ds(pl.multiple_of(i * 16, 16), 16), :] = (x * inv * gain_row).astype(BF16)
        return carry

    lax.fori_loop(0, 32, norm, 0)
    ffn[0].wait()
    ffn[1].wait()

    def up(i, carry):
        at = pl.ds(pl.multiple_of(i * 256, 256), 256)
        gate = jnp.dot(xs[...], gw[:, at], preferred_element_type=F32)
        upper = jnp.dot(xs[...], uw[:, at], preferred_element_type=F32)
        hid[:, at] = (gate / (1.0 + jnp.exp(-gate)) * upper).astype(BF16)
        return carry

    lax.fori_loop(0, 3, up, 0)
    ffn[2].wait()

    def back_copy(i, pp, h):
        tp = lax.rem(p + pp, 8)
        te = lax.rem(chip + i, 8) * 2 + lax.rem(core + h, 2)
        return pltpu.make_async_remote_copy(
            src_ref=ybuf.at[tp * 16 + te],
            dst_ref=zbuf.at[me],
            send_sem=back_s,
            recv_sem=back_r.at[i],
            device_id={"pool": tp, "expert": te},
            device_id_type=MESH,
        )

    def send_back(i, own):
        for pp in range(8):
            for h in range(2):
                if not (own and pp == 0 and h == 0):
                    back_copy(i, pp, h).start()

    def down(i):
        tile = lax.rem(chip + i, 8)
        at = pl.ds(pl.multiple_of(tile * 256, 256), 256)
        y = jnp.dot(hid[...], dw[:, at], preferred_element_type=F32).astype(BF16)
        for pp in range(8):
            for h in range(2):
                ybuf[pp * 16 + tile * 2 + h] = y[
                    pp * SLOTS : (pp + 1) * SLOTS, h * HD : (h + 1) * HD
                ]

    down(0)
    down(1)
    send_back(0, True)

    def downs(i, carry):
        down(i)
        send_back(i - 1, False)
        return carry

    lax.fori_loop(2, 8, downs, 0)
    send_back(7, False)
    zbuf[me] = ybuf[me]

    mixt[...] = jnp.zeros_like(mixt)

    def gather_back(i, carry):
        first = lax.rem(chip + 8 - i, 8) * 2
        for c in range(4):
            parts, ys = [], []
            for pp in (2 * c, 2 * c + 1):
                for h in range(2):
                    t = pp * 16 + first + h
                    parts.append(
                        jnp.where(
                            slot_ref[pl.ds(t, 1), :] == place, wt_ref[pl.ds(t, 1), :], 0.0
                        ).astype(BF16)
                    )
                    ys.append(zbuf[t])
            chosen = jnp.concatenate(parts, axis=0)
            y = jnp.concatenate(ys, axis=0)
            mixt[...] += lax.dot_general(y, chosen, TN, preferred_element_type=F32)
        return carry

    def back_all(i, number):
        return pltpu.make_async_remote_copy(
            src_ref=ybuf.at[pl.ds(0, number)],
            dst_ref=zbuf.at[pl.ds(0, number)],
            send_sem=back_s,
            recv_sem=back_r.at[i],
            device_id={"pool": p, "expert": sib},
            device_id_type=MESH,
        )

    back_all(0, 15).wait_recv()
    gather_back(0, 0)

    def collect(i, carry):
        back_all(i, 16).wait_recv()
        return gather_back(i, carry)

    lax.fori_loop(1, 8, collect, 0)
    mix_ref[...] = mixt[...].T.astype(BF16)
    out_all.wait_send()
    back_all(0, 127).wait_send()
    for g in range(4):
        own_y(g).wait_send()
        for kind in range(4):
            z_copy(kind, g, 0).wait_send()
            z_copy(kind, g, 1).wait_send()
    send_w.wait_send()
    send_res.wait_send()
    send_out.wait_send()


def shards(
    queries,
    kv_cache,
    block_index,
    lengths,
    residual,
    out_weight,
    norm_gain,
    expert_ids,
    route_weights,
    gate_weight,
    up_weight,
    down_weight,
):
    rows = queries.shape[0]
    span = kv_cache.shape[0] * kv_cache.shape[1]
    width = kv_cache.shape[2]
    wide, hidden = gate_weight.shape[1:]
    dma = pltpu.SemaphoreType.DMA
    att, mixed = pl.pallas_call(
        layer,
        out_shape=(
            jax.ShapeDtypeStruct((8, 2, 32, HD), BF16),
            jax.ShapeDtypeStruct((512, HD), BF16),
        ),
        in_specs=[VM, ANY, VM, VM, VM, ANY, VM, VM, VM, ANY, ANY, ANY],
        out_specs=(VM, VM),
        scratch_shapes=[
            pltpu.VMEM((width // HD, span, HD), BF16),
            pltpu.VMEM(out_weight.shape, BF16),
            pltpu.VMEM(out_weight.shape, BF16),
            pltpu.VMEM((8, 32, HD), BF16),
            pltpu.VMEM((8, 4, 32, 8 * HD), BF16),
            pltpu.VMEM((256, span), F32),
            pltpu.VMEM((256, span), BF16),
            pltpu.VMEM((256, HD), F32),
            pltpu.VMEM((rows, span), F32),
            pltpu.VMEM((8, 32, HD), BF16),
            pltpu.VMEM((2, 256, HD), F32),
            pltpu.VMEM((128, 128), jnp.int32),
            pltpu.VMEM((16, 1, HD), F32),
            pltpu.VMEM((128, 512), F32),
            pltpu.VMEM((128, 512), F32),
            pltpu.VMEM((wide, hidden), BF16),
            pltpu.VMEM((wide, hidden), BF16),
            pltpu.VMEM((hidden, wide), BF16),
            pltpu.VMEM((128, SLOTS, HD), BF16),
            pltpu.VMEM((128, SLOTS, HD), BF16),
            pltpu.VMEM((128, SLOTS, HD), BF16),
            pltpu.VMEM((128, SLOTS, HD), BF16),
            pltpu.VMEM((512, wide), BF16),
            pltpu.VMEM((512, hidden), BF16),
            pltpu.VMEM((HD, 512), F32),
            dma((8,)),
            dma,
            dma((4,)),
            dma((4,)),
            dma((4, 4, 2)),
            dma((4, 4, 2)),
            dma((3,)),
            dma((3,)),
            dma((16,)),
            dma((16,)),
            dma((3,)),
            dma,
            dma,
            dma,
            dma((8,)),
        ],
        compiler_params=pltpu.CompilerParams(
            collective_id=0, has_side_effects=True, vmem_limit_bytes=60 * 1024 * 1024
        ),
        name="layer",
    )(
        queries,
        kv_cache.reshape(span, width),
        block_index.T,
        lengths.reshape(1, rows),
        residual.reshape(8, 2, 32, HD),
        out_weight,
        norm_gain.reshape(1, HD),
        expert_ids.T,
        route_weights.T,
        gate_weight,
        up_weight,
        down_weight,
    )
    return (att.reshape(512, HD), mixed)


def solution(mesh):
    return jax.shard_map(
        shards,
        mesh=mesh,
        in_specs=(
            P(("pool", "expert"), None),
            P(("pool", "expert"), None, None),
            P(("pool", "expert"), None),
            P(("pool", "expert")),
            P("pool", "expert"),
            P(None, "expert"),
            P("expert"),
            P("pool", None),
            P("pool", None),
            P(("pool", "expert"), None, None),
            P(("pool", "expert"), None, None),
            P(("pool", "expert"), None, None),
        ),
        out_specs=(P("pool", "expert"), P("pool", "expert")),
        check_vma=False,
    )
```

```python
import math

import jax
import jax.numpy as jnp
from jax import lax
from jax.experimental import pallas as pl
from jax.experimental.pallas import tpu as pltpu
from jax.sharding import PartitionSpec as P

HD = 128
EPS = 1e-06
MESH = pl.DeviceIdType.MESH
F32 = jnp.float32
BF16 = jnp.bfloat16
VM = pl.BlockSpec(memory_space=pltpu.VMEM)
ANY = pl.BlockSpec(memory_space=pl.ANY)
NT = (((1,), (1,)), ((), ()))
TN = (((0,), (0,)), ((), ()))
SLOTS = 64


def layer(
    q_ref,
    kv_hbm,
    bi_ref,
    len_ref,
    res_ref,
    w_hbm,
    gain_ref,
    ids_ref,
    rw_ref,
    g_hbm,
    u_hbm,
    d_hbm,
    att_ref,
    mix_ref,
    kv,
    wown,
    wsib,
    ressib,
    gath,
    s_scr,
    p_scr,
    linv,
    bias,
    stage,
    acc,
    table,
    gall_ref,
    slot_ref,
    wt_ref,
    gw,
    uw,
    dw,
    obuf,
    rbuf,
    ybuf,
    zbuf,
    xs,
    hid,
    mixt,
    in_sem,
    w_sem,
    y_s,
    y_r,
    z_s,
    z_r,
    sib_s,
    sib_r,
    gain_s,
    gain_r,
    ffn_sem,
    out_s,
    out_r,
    back_s,
    back_r,
):
    p = lax.axis_index("pool")
    e = lax.axis_index("expert")
    core = e % 2
    chip = e // 2
    y_hi = chip // 4
    z = chip % 4
    sib = e + 1 - 2 * core
    chip_y = chip + 4 - 8 * y_hi
    z_up = (z + 1) % 4
    z_dn = (z + 3) % 4
    z_op = (z + 2) % 4
    chip_up = y_hi * 4 + z_up
    chip_dn = y_hi * 4 + z_dn
    chip_op = y_hi * 4 + z_op
    flip = 4 - 8 * y_hi
    dev_y = chip_y * 2 + core
    dev_up = chip_up * 2 + core
    dev_dn = chip_dn * 2 + core

    me = p * 16 + e
    barrier = pltpu.get_barrier_semaphore()

    def fetch(i):
        return pltpu.make_async_copy(kv_hbm.at[:, pl.ds(i * HD, HD)], kv.at[i], in_sem.at[i])

    fetch_w = pltpu.make_async_copy(w_hbm, wown, w_sem)
    for g in range(4):
        fetch(g).start()
        fetch(4 + g).start()
    ffn = [
        pltpu.make_async_copy(g_hbm.at[0], gw, ffn_sem.at[0]),
        pltpu.make_async_copy(u_hbm.at[0], uw, ffn_sem.at[1]),
        pltpu.make_async_copy(d_hbm.at[0], dw, ffn_sem.at[2]),
    ]

    def greet(d, carry):
        t = lax.rem(me + d, 128)
        pl.semaphore_signal(
            barrier,
            inc=1,
            device_id={"pool": lax.div(t, 16), "expert": lax.rem(t, 16)},
            device_id_type=MESH,
        )
        return carry

    lax.fori_loop(1, 128, greet, 0)

    rows, span = bias.shape
    lane = lax.broadcasted_iota(jnp.int32, (rows, span), 1)
    block = lane // 64
    offset = lane % 64
    count = jnp.zeros((rows, span), F32)
    table[...] = jnp.zeros_like(table)
    table[0:8, 0:rows] = bi_ref[...]
    table[8:16, 0:rows] = jnp.broadcast_to(len_ref[...], (8, rows))
    turned = table[...].T[0:rows, :]
    for j in range(8):
        live = (block == turned[:, j : j + 1]) & (offset < turned[:, 8:9] - 64 * j)
        count = count + jnp.where(live, 1.0, 0.0)
    bias[...] = jnp.where(count > 0.0, jnp.log2(jnp.maximum(count, 1.0)), -1e30)

    factor = HD ** (-0.5) * math.log2(math.e)

    def attend(g):
        fetch(g).wait()
        query = jnp.concatenate(
            [q_ref[:, (g * 8 + i) * HD : (g * 8 + i + 1) * HD] for i in range(8)], axis=0
        )
        s_scr[...] = lax.dot_general(query, kv[g], NT, preferred_element_type=F32)

        def soften(r, carry):
            for v in range(4):
                at = pl.ds(pl.multiple_of(r * 64 + v * 16, 16), 16)
                x = s_scr[at, :] * factor + bias[(v % 2) * 16 : (v % 2) * 16 + 16, :]
                top = jnp.max(x, axis=1, keepdims=True)
                ex = jnp.exp2(x - top)
                total = jnp.sum(ex, axis=1, keepdims=True)
                p_scr[at, :] = ex.astype(BF16)
                linv[at, :] = jnp.broadcast_to(1.0 / total, (16, HD))
            return carry

        lax.fori_loop(0, 4, soften, 0)
        fetch(4 + g).wait()
        o = jnp.dot(p_scr[...], kv[4 + g], preferred_element_type=F32) * linv[...]
        o = o.astype(BF16)
        for i in range(8):
            gath[chip, g, :, i * HD : (i + 1) * HD] = o[i * 32 : (i + 1) * 32]

    def remote(src, dst, ssem, rsem, dev):
        return pltpu.make_async_remote_copy(
            src_ref=src,
            dst_ref=dst,
            send_sem=ssem,
            recv_sem=rsem,
            device_id={"expert": dev},
            device_id_type=MESH,
        )

    lo, hi = pl.ds(0, 16), pl.ds(16, 16)

    def block_copy(c, g, ssem, rsem, dev, part=None):
        ref = gath.at[c, g] if part is None else gath.at[c, g, part]
        return remote(ref, ref, ssem, rsem, dev)

    def own_y(g):
        return block_copy(chip, g, y_s.at[g], y_r.at[g], dev_y)

    def z_copy(kind, g, way):
        dev = dev_up if way == 0 else dev_dn
        ss, rs = z_s.at[kind, g, way], z_r.at[kind, g, way]
        if kind == 0:
            return block_copy(chip, g, ss, rs, dev)
        if kind == 1:
            return block_copy(chip_y, g, ss, rs, dev)
        source = chip_dn if way == 0 else chip_up
        if kind == 3:
            source = source + flip
        return block_copy(source, g, ss, rs, dev, lo if way == 0 else hi)

    def send_own(g):
        z_copy(0, g, 0).start()
        z_copy(0, g, 1).start()
        own_y(g).start()

    def send_partner(g):
        own_y(g).wait_recv()
        z_copy(1, g, 0).start()
        z_copy(1, g, 1).start()

    def relay(kind, g):
        for way in (0, 1):
            z_copy(kind, g, way).wait_recv()
            z_copy(kind + 2, g, way).start()

    def finish(g):
        for way in (0, 1):
            z_copy(2, g, way).wait_recv()
            z_copy(3, g, way).wait_recv()

    def project(g):
        depth = 8 * HD
        at = pl.ds(g * depth, depth)
        rows_g = gath[:, g].reshape(256, depth)
        part = jnp.dot(rows_g, wown[at, :], preferred_element_type=F32)
        other = jnp.dot(rows_g, wsib[at, :], preferred_element_type=F32)
        if g == 0:
            acc[0] = part
            acc[1] = other
        else:
            acc[0] += part
            acc[1] += other

    attend(0)
    fetch_w.start()
    pl.semaphore_wait(barrier, 127)
    send_own(0)
    send_w = remote(w_hbm, wsib, sib_s.at[0], sib_r.at[0], sib)
    send_w.start()
    send_res = remote(res_ref.at[:, 1 - core], ressib, sib_s.at[1], sib_r.at[1], sib)
    send_res.start()
    gall_ref[e] = gain_ref[...]
    gains = [
        remote(gain_ref, gall_ref.at[e], gain_s.at[d], gain_r.at[d], (e + d) % 16)
        for d in range(1, 16)
    ]
    for gain in gains:
        gain.start()
    attend(1)
    for copy in ffn:
        copy.start()
    send_own(1)
    send_partner(0)
    relay(0, 0)
    attend(2)
    send_own(2)
    relay(1, 0)
    send_partner(1)
    relay(0, 1)
    attend(3)
    send_own(3)
    relay(1, 1)
    send_partner(2)
    relay(0, 2)
    experts, seqs = slot_ref.shape
    which = lax.broadcasted_iota(jnp.int32, (experts, seqs), 0)
    named = jnp.zeros((experts, seqs), F32)
    weight = jnp.zeros((experts, seqs), F32)
    for k in range(8):
        same = which == ids_ref[k : k + 1, :]
        named = named + jnp.where(same, 1.0, 0.0)
        weight = weight + jnp.where(same, rw_ref[k : k + 1, :], 0.0)
    wt_ref[...] = weight
    early = lax.broadcasted_iota(jnp.int32, (seqs, seqs), 0)
    late = lax.broadcasted_iota(jnp.int32, (seqs, seqs), 1)
    ahead = jnp.where(early < late, 1.0, 0.0).astype(BF16)
    slots = jnp.dot(named.astype(BF16), ahead, preferred_element_type=F32)
    slot_ref[...] = jnp.where(named > 0.0, slots, -1.0)
    fetch_w.wait()
    send_w.wait_recv()
    finish(0)
    project(0)
    relay(1, 2)
    send_partner(3)
    relay(0, 3)
    finish(1)
    project(1)
    relay(1, 3)
    finish(2)
    project(2)
    finish(3)
    project(3)
    send_res.wait_recv()
    stage[...] = (ressib[...].astype(F32) + acc[1].reshape(8, 32, HD)).astype(BF16)
    send_out = remote(stage, att_ref.at[:, core], sib_s.at[2], sib_r.at[2], sib)
    send_out.start()
    att_ref[:, core] = (res_ref[:, core].astype(F32) + acc[0].reshape(8, 32, HD)).astype(BF16)
    send_out.wait_recv()

    place = lax.broadcasted_iota(jnp.int32, (SLOTS, seqs), 0).astype(F32)
    px, py = p // 2, p % 2

    def place_of(xx, yl, yh, zz, c):
        return (xx * 2 + yl) * 16 + yh * 8 + zz * 2 + c

    def digits(d):
        d = lax.rem(d * 37, 64)
        c = lax.rem(d, 2)
        d = lax.div(d, 2)
        dz = lax.rem(d, 4)
        d = lax.div(d, 4)
        dh = lax.rem(d, 2)
        d = lax.div(d, 2)
        return c, dz, dh, lax.rem(d, 2), lax.div(d, 2)

    def target(half, d):
        c, dz, dh, dl, dx = digits(d)
        return place_of(
            lax.rem(px + 2 * dx + half, 4),
            lax.rem(py + dl, 2),
            lax.rem(y_hi + dh, 2),
            lax.rem(z + dz, 4),
            lax.rem(core + c, 2),
        )

    def origin(half, d):
        c, dz, dh, dl, dx = digits(d)
        return place_of(
            lax.rem(px + 8 - 2 * dx - half, 4),
            lax.rem(py + dl, 2),
            lax.rem(y_hi + dh, 2),
            lax.rem(z + 4 - dz, 4),
            lax.rem(core + c, 2),
        )

    def send_to(t, src, dst, ssem, rsem):
        return pltpu.make_async_remote_copy(
            src_ref=src,
            dst_ref=dst,
            send_sem=ssem,
            recv_sem=rsem,
            device_id={"pool": lax.div(t, 16), "expert": lax.rem(t, 16)},
            device_id_type=MESH,
        )

    def out_copy(half, d):
        t = target(half, d)
        return send_to(t, obuf.at[t], rbuf.at[me], out_s, out_r.at[half])

    def pick(half, i):
        places, parts = [], []
        for u in range(4):
            t = target(half, i * 4 + u)
            places.append(t)
            parts.append(jnp.where(slot_ref[pl.ds(t, 1), :] == place, 1.0, 0.0).astype(BF16))
        chosen = jnp.concatenate(parts, axis=0)
        picked = jnp.dot(chosen, att_ref[...].reshape(seqs, HD), preferred_element_type=F32)
        return places, picked.astype(BF16)

    places, picked = pick(0, 0)
    rbuf[me] = picked[0:SLOTS]
    for u in range(1, 4):
        obuf[places[u]] = picked[u * SLOTS : (u + 1) * SLOTS]

    def some(half):
        def step(i, carry):
            places, picked = pick(half, i)
            for u in range(4):
                obuf[places[u]] = picked[u * SLOTS : (u + 1) * SLOTS]
            for u in range(4):
                out_copy(half, i * 4 + u - 3).start()
            return carry

        return step

    lax.fori_loop(1, 16, some(0), 0)
    for u in range(61, 64):
        out_copy(0, u).start()
    places, picked = pick(1, 0)
    for u in range(4):
        obuf[places[u]] = picked[u * SLOTS : (u + 1) * SLOTS]
    out_copy(1, 0).start()
    lax.fori_loop(1, 16, some(1), 0)
    for u in range(61, 64):
        out_copy(1, u).start()

    def many(src, dst, ssem, rsem, number):
        return send_to(
            p * 16 + sib, src.at[pl.ds(0, number)], dst.at[pl.ds(0, number)], ssem, rsem
        )

    for gain in gains:
        gain.wait()
    gain_row = jnp.concatenate([gall_ref[f] for f in range(16)], axis=1)

    def back_copy(half, d):
        t = target(half, d)
        return send_to(t, ybuf.at[t], zbuf.at[me], back_s, back_r.at[half * 4 + lax.div(d, 16)])

    def experts_of(half):
        low = lax.rem(px + half, 2) * 2
        many(obuf, rbuf, out_s, out_r.at[half], 63 + half).wait_recv()

        def norm(i, carry):
            q = lax.div(i, 4)
            first = (low + lax.rem(q, 2) + lax.div(q, 2) * 4) * 16
            at = pl.ds(pl.multiple_of(lax.rem(i, 4) * 16, 16), 16)
            x = jnp.concatenate([rbuf[first + f, at, :] for f in range(16)], axis=1).astype(F32)
            inv = lax.rsqrt(jnp.sum(x * x, axis=1, keepdims=True) / (16 * HD) + EPS)
            xs[pl.ds(pl.multiple_of(i * 16, 16), 16), :] = (x * inv * gain_row).astype(BF16)
            return carry

        lax.fori_loop(0, 16, norm, 0)
        if half == 0:
            ffn[0].wait()
            ffn[1].wait()

        def up(i, carry):
            at = pl.ds(pl.multiple_of(i * 256, 256), 256)
            gate = jnp.dot(xs[...], gw[:, at], preferred_element_type=F32)
            upper = jnp.dot(xs[...], uw[:, at], preferred_element_type=F32)
            hid[:, at] = (gate / (1.0 + jnp.exp(-gate)) * upper).astype(BF16)
            return carry

        lax.fori_loop(0, 3, up, 0)
        if half == 0:
            ffn[2].wait()

        def down(tile, carry):
            at = pl.ds(pl.multiple_of(tile * 256, 256), 256)
            y = jnp.dot(hid[...], dw[:, at], preferred_element_type=F32).astype(BF16)
            for q in range(4):
                first = (low + q % 2 + (q // 2) * 4) * 16
                for h in range(2):
                    ybuf[first + tile * 2 + h] = y[
                        q * SLOTS : (q + 1) * SLOTS, h * HD : (h + 1) * HD
                    ]
            return carry

        lax.fori_loop(0, 8, down, 0)

        def send(d, carry):
            back_copy(half, d).start()
            return carry

        lax.fori_loop(1 - half, 64, send, 0)

    experts_of(0)
    experts_of(1)
    zbuf[me] = ybuf[me]

    mixt[...] = jnp.zeros_like(mixt)

    def gather_back(half, k):
        many(ybuf, zbuf, back_s, back_r.at[half * 4 + k], 15 if half + k == 0 else 16).wait_recv()

        def four(c, carry):
            parts, ys = [], []
            for u in range(4):
                t = origin(half, k * 16 + c * 4 + u)
                parts.append(
                    jnp.where(
                        slot_ref[pl.ds(t, 1), :] == place, wt_ref[pl.ds(t, 1), :], 0.0
                    ).astype(BF16)
                )
                ys.append(zbuf[t])
            chosen = jnp.concatenate(parts, axis=0)
            y = jnp.concatenate(ys, axis=0)
            mixt[...] += lax.dot_general(y, chosen, TN, preferred_element_type=F32)
            return carry

        lax.fori_loop(0, 4, four, 0)

    for half in range(2):
        for k in range(4):
            gather_back(half, k)
    mix_ref[...] = mixt[...].T.astype(BF16)
    many(obuf, rbuf, out_s, out_r.at[0], 127).wait_send()
    many(ybuf, zbuf, back_s, back_r.at[0], 127).wait_send()
    for g in range(4):
        own_y(g).wait_send()
        for kind in range(4):
            z_copy(kind, g, 0).wait_send()
            z_copy(kind, g, 1).wait_send()
    send_w.wait_send()
    send_res.wait_send()
    send_out.wait_send()


def shards(
    queries,
    kv_cache,
    block_index,
    lengths,
    residual,
    out_weight,
    norm_gain,
    expert_ids,
    route_weights,
    gate_weight,
    up_weight,
    down_weight,
):
    rows = queries.shape[0]
    span = kv_cache.shape[0] * kv_cache.shape[1]
    width = kv_cache.shape[2]
    wide, hidden = gate_weight.shape[1:]
    dma = pltpu.SemaphoreType.DMA
    att, mixed = pl.pallas_call(
        layer,
        out_shape=(
            jax.ShapeDtypeStruct((8, 2, 32, HD), BF16),
            jax.ShapeDtypeStruct((512, HD), BF16),
        ),
        in_specs=[VM, ANY, VM, VM, VM, ANY, VM, VM, VM, ANY, ANY, ANY],
        out_specs=(VM, VM),
        scratch_shapes=[
            pltpu.VMEM((width // HD, span, HD), BF16),
            pltpu.VMEM(out_weight.shape, BF16),
            pltpu.VMEM(out_weight.shape, BF16),
            pltpu.VMEM((8, 32, HD), BF16),
            pltpu.VMEM((8, 4, 32, 8 * HD), BF16),
            pltpu.VMEM((256, span), F32),
            pltpu.VMEM((256, span), BF16),
            pltpu.VMEM((256, HD), F32),
            pltpu.VMEM((rows, span), F32),
            pltpu.VMEM((8, 32, HD), BF16),
            pltpu.VMEM((2, 256, HD), F32),
            pltpu.VMEM((128, 128), jnp.int32),
            pltpu.VMEM((16, 1, HD), F32),
            pltpu.VMEM((128, 512), F32),
            pltpu.VMEM((128, 512), F32),
            pltpu.VMEM((wide, hidden), BF16),
            pltpu.VMEM((wide, hidden), BF16),
            pltpu.VMEM((hidden, wide), BF16),
            pltpu.VMEM((128, SLOTS, HD), BF16),
            pltpu.VMEM((128, SLOTS, HD), BF16),
            pltpu.VMEM((128, SLOTS, HD), BF16),
            pltpu.VMEM((128, SLOTS, HD), BF16),
            pltpu.VMEM((256, wide), BF16),
            pltpu.VMEM((256, hidden), BF16),
            pltpu.VMEM((HD, 512), F32),
            dma((8,)),
            dma,
            dma((4,)),
            dma((4,)),
            dma((4, 4, 2)),
            dma((4, 4, 2)),
            dma((3,)),
            dma((3,)),
            dma((16,)),
            dma((16,)),
            dma((3,)),
            dma,
            dma((2,)),
            dma,
            dma((8,)),
        ],
        compiler_params=pltpu.CompilerParams(
            collective_id=0, has_side_effects=True, vmem_limit_bytes=60 * 1024 * 1024
        ),
        name="layer",
    )(
        queries,
        kv_cache.reshape(span, width),
        block_index.T,
        lengths.reshape(1, rows),
        residual.reshape(8, 2, 32, HD),
        out_weight,
        norm_gain.reshape(1, HD),
        expert_ids.T,
        route_weights.T,
        gate_weight,
        up_weight,
        down_weight,
    )
    return (att.reshape(512, HD), mixed)


def solution(mesh):
    return jax.shard_map(
        shards,
        mesh=mesh,
        in_specs=(
            P(("pool", "expert"), None),
            P(("pool", "expert"), None, None),
            P(("pool", "expert"), None),
            P(("pool", "expert")),
            P("pool", "expert"),
            P(None, "expert"),
            P("expert"),
            P("pool", None),
            P("pool", None),
            P(("pool", "expert"), None, None),
            P(("pool", "expert"), None, None),
            P(("pool", "expert"), None, None),
        ),
        out_specs=(P("pool", "expert"), P("pool", "expert")),
        check_vma=False,
    )
```

```python
import math

import jax
import jax.numpy as jnp
from jax import lax
from jax.experimental import pallas as pl
from jax.experimental.pallas import tpu as pltpu
from jax.sharding import PartitionSpec as P

HD = 128
EPS = 1e-06
MESH = pl.DeviceIdType.MESH
F32 = jnp.float32
BF16 = jnp.bfloat16
VM = pl.BlockSpec(memory_space=pltpu.VMEM)
ANY = pl.BlockSpec(memory_space=pl.ANY)
NT = (((1,), (1,)), ((), ()))
TN = (((0,), (0,)), ((), ()))
SLOTS = 64


def layer(
    q_ref,
    kv_hbm,
    bi_ref,
    len_ref,
    res_ref,
    w_hbm,
    gain_ref,
    ids_ref,
    rw_ref,
    g_hbm,
    u_hbm,
    d_hbm,
    att_ref,
    mix_ref,
    kv,
    wown,
    wsib,
    ressib,
    gath,
    s_scr,
    p_scr,
    linv,
    bias,
    stage,
    acc,
    table,
    gall_ref,
    slot_ref,
    wt_ref,
    gw,
    uw,
    dw,
    obuf,
    rbuf,
    ybuf,
    zbuf,
    xs,
    hid,
    mixt,
    in_sem,
    w_sem,
    y_s,
    y_r,
    z_s,
    z_r,
    sib_s,
    sib_r,
    gain_s,
    gain_r,
    ffn_sem,
    out_s,
    out_r,
    back_s,
    back_r,
    ym_s,
    ym_r,
):
    p = lax.axis_index("pool")
    e = lax.axis_index("expert")
    core = e % 2
    chip = e // 2
    y_hi = chip // 4
    z = chip % 4
    sib = e + 1 - 2 * core
    chip_y = chip + 4 - 8 * y_hi
    z_up = (z + 1) % 4
    z_dn = (z + 3) % 4
    z_op = (z + 2) % 4
    chip_up = y_hi * 4 + z_up
    chip_dn = y_hi * 4 + z_dn
    chip_op = y_hi * 4 + z_op
    flip = 4 - 8 * y_hi
    dev_y = chip_y * 2 + core
    dev_up = chip_up * 2 + core
    dev_dn = chip_dn * 2 + core

    me = p * 16 + e
    barrier = pltpu.get_barrier_semaphore()

    def fetch(i):
        return pltpu.make_async_copy(kv_hbm.at[:, pl.ds(i * HD, HD)], kv.at[i], in_sem.at[i])

    fetch_w = pltpu.make_async_copy(w_hbm, wown, w_sem)
    for g in range(4):
        fetch(g).start()
        fetch(4 + g).start()
    ffn = [
        pltpu.make_async_copy(g_hbm.at[0], gw, ffn_sem.at[0]),
        pltpu.make_async_copy(u_hbm.at[0], uw, ffn_sem.at[1]),
        pltpu.make_async_copy(d_hbm.at[0], dw, ffn_sem.at[2]),
    ]

    def greet(d, carry):
        t = lax.rem(me + d, 128)
        pl.semaphore_signal(
            barrier,
            inc=1,
            device_id={"pool": lax.div(t, 16), "expert": lax.rem(t, 16)},
            device_id_type=MESH,
        )
        return carry

    lax.fori_loop(1, 128, greet, 0)

    rows, span = bias.shape
    lane = lax.broadcasted_iota(jnp.int32, (rows, span), 1)
    block = lane // 64
    offset = lane % 64
    count = jnp.zeros((rows, span), F32)
    table[...] = jnp.zeros_like(table)
    table[0:8, 0:rows] = bi_ref[...]
    table[8:16, 0:rows] = jnp.broadcast_to(len_ref[...], (8, rows))
    turned = table[...].T[0:rows, :]
    for j in range(8):
        live = (block == turned[:, j : j + 1]) & (offset < turned[:, 8:9] - 64 * j)
        count = count + jnp.where(live, 1.0, 0.0)
    bias[...] = jnp.where(count > 0.0, jnp.log2(jnp.maximum(count, 1.0)), -1e30)

    factor = HD ** (-0.5) * math.log2(math.e)

    def attend(g):
        fetch(g).wait()
        query = jnp.concatenate(
            [q_ref[:, (g * 8 + i) * HD : (g * 8 + i + 1) * HD] for i in range(8)], axis=0
        )
        s_scr[...] = lax.dot_general(query, kv[g], NT, preferred_element_type=F32)

        def soften(r, carry):
            for v in range(4):
                at = pl.ds(pl.multiple_of(r * 64 + v * 16, 16), 16)
                x = s_scr[at, :] * factor + bias[(v % 2) * 16 : (v % 2) * 16 + 16, :]
                top = jnp.max(x, axis=1, keepdims=True)
                ex = jnp.exp2(x - top)
                total = jnp.sum(ex, axis=1, keepdims=True)
                p_scr[at, :] = ex.astype(BF16)
                linv[at, :] = jnp.broadcast_to(1.0 / total, (16, HD))
            return carry

        lax.fori_loop(0, 4, soften, 0)
        fetch(4 + g).wait()
        o = jnp.dot(p_scr[...], kv[4 + g], preferred_element_type=F32) * linv[...]
        o = o.astype(BF16)
        for i in range(8):
            gath[chip, g, :, i * HD : (i + 1) * HD] = o[i * 32 : (i + 1) * 32]

    def remote(src, dst, ssem, rsem, dev):
        return pltpu.make_async_remote_copy(
            src_ref=src,
            dst_ref=dst,
            send_sem=ssem,
            recv_sem=rsem,
            device_id={"expert": dev},
            device_id_type=MESH,
        )

    lo, hi = pl.ds(0, 16), pl.ds(16, 16)

    def block_copy(c, g, ssem, rsem, dev, part=None):
        ref = gath.at[c, g] if part is None else gath.at[c, g, part]
        return remote(ref, ref, ssem, rsem, dev)

    def own_y(g):
        return block_copy(chip, g, y_s.at[g], y_r.at[g], dev_y)

    def z_copy(kind, g, way):
        dev = dev_up if way == 0 else dev_dn
        ss, rs = z_s.at[kind, g, way], z_r.at[kind, g, way]
        if kind == 0:
            return block_copy(chip, g, ss, rs, dev)
        if kind == 1:
            return block_copy(chip_y, g, ss, rs, dev)
        source = chip_dn if way == 0 else chip_up
        if kind == 3:
            source = source + flip
        return block_copy(source, g, ss, rs, dev, lo if way == 0 else hi)

    def send_own(g):
        z_copy(0, g, 0).start()
        z_copy(0, g, 1).start()
        own_y(g).start()

    def send_partner(g):
        own_y(g).wait_recv()
        z_copy(1, g, 0).start()
        z_copy(1, g, 1).start()

    def relay(kind, g):
        for way in (0, 1):
            z_copy(kind, g, way).wait_recv()
            z_copy(kind + 2, g, way).start()

    def finish(g):
        for way in (0, 1):
            z_copy(2, g, way).wait_recv()
            z_copy(3, g, way).wait_recv()

    def y_more(kind, g):
        ss, rs = ym_s.at[kind, g], ym_r.at[kind, g]
        if kind < 2:
            return block_copy(chip_up if kind else chip_dn, g, ss, rs, dev_y)
        return block_copy(chip_op, g, ss, rs, dev_y, hi if kind == 3 else lo)

    def first_z(g):
        for way in (0, 1):
            z_copy(0, g, way).wait_recv()
            z_copy(2, g, way).start()
            y_more(way, g).start()

    def second_z(g):
        for way in (0, 1):
            z_copy(2, g, way).wait_recv()
            y_more(2 + way, g).start()

    def finish_y(g):
        own_y(g).wait_recv()
        for kind in range(4):
            y_more(kind, g).wait_recv()

    def project(g):
        depth = 8 * HD
        at = pl.ds(g * depth, depth)
        rows_g = gath[:, g].reshape(256, depth)
        part = jnp.dot(rows_g, wown[at, :], preferred_element_type=F32)
        other = jnp.dot(rows_g, wsib[at, :], preferred_element_type=F32)
        if g == 0:
            acc[0] = part
            acc[1] = other
        else:
            acc[0] += part
            acc[1] += other

    attend(0)
    fetch_w.start()
    pl.semaphore_wait(barrier, 127)
    send_own(0)
    send_w = remote(w_hbm, wsib, sib_s.at[0], sib_r.at[0], sib)
    send_w.start()
    send_res = remote(res_ref.at[:, 1 - core], ressib, sib_s.at[1], sib_r.at[1], sib)
    send_res.start()
    gall_ref[e] = gain_ref[...]
    gains = [
        remote(gain_ref, gall_ref.at[e], gain_s.at[d], gain_r.at[d], (e + d) % 16)
        for d in range(1, 16)
    ]
    for gain in gains:
        gain.start()
    attend(1)
    for copy in ffn:
        copy.start()
    send_own(1)
    attend(2)
    send_own(2)
    first_z(0)
    attend(3)
    send_own(3)
    first_z(1)
    second_z(0)
    send_partner(2)
    experts, seqs = slot_ref.shape
    which = lax.broadcasted_iota(jnp.int32, (experts, seqs), 0)
    named = jnp.zeros((experts, seqs), F32)
    weight = jnp.zeros((experts, seqs), F32)
    for k in range(8):
        same = which == ids_ref[k : k + 1, :]
        named = named + jnp.where(same, 1.0, 0.0)
        weight = weight + jnp.where(same, rw_ref[k : k + 1, :], 0.0)
    wt_ref[...] = weight
    early = lax.broadcasted_iota(jnp.int32, (seqs, seqs), 0)
    late = lax.broadcasted_iota(jnp.int32, (seqs, seqs), 1)
    ahead = jnp.where(early < late, 1.0, 0.0).astype(BF16)
    slots = jnp.dot(named.astype(BF16), ahead, preferred_element_type=F32)
    slot_ref[...] = jnp.where(named > 0.0, slots, -1.0)
    relay(0, 2)
    second_z(1)
    send_partner(3)
    fetch_w.wait()
    send_w.wait_recv()
    relay(0, 3)
    relay(1, 2)
    finish_y(0)
    project(0)
    relay(1, 3)
    finish_y(1)
    project(1)
    finish(2)
    project(2)
    finish(3)
    project(3)
    send_res.wait_recv()
    stage[...] = (ressib[...].astype(F32) + acc[1].reshape(8, 32, HD)).astype(BF16)
    send_out = remote(stage, att_ref.at[:, core], sib_s.at[2], sib_r.at[2], sib)
    send_out.start()
    att_ref[:, core] = (res_ref[:, core].astype(F32) + acc[0].reshape(8, 32, HD)).astype(BF16)
    send_out.wait_recv()

    place = lax.broadcasted_iota(jnp.int32, (SLOTS, seqs), 0).astype(F32)
    px, py = p // 2, p % 2

    def place_of(xx, yl, yh, zz, c):
        return (xx * 2 + yl) * 16 + yh * 8 + zz * 2 + c

    def digits(d):
        d = lax.rem(d * 37, 64)
        c = lax.rem(d, 2)
        d = lax.div(d, 2)
        dz = lax.rem(d, 4)
        d = lax.div(d, 4)
        dh = lax.rem(d, 2)
        d = lax.div(d, 2)
        return c, dz, dh, lax.rem(d, 2), lax.div(d, 2)

    def target(half, d):
        c, dz, dh, dl, dx = digits(d)
        return place_of(
            lax.rem(px + 2 * dx + half, 4),
            lax.rem(py + dl, 2),
            lax.rem(y_hi + dh, 2),
            lax.rem(z + dz, 4),
            lax.rem(core + c, 2),
        )

    def origin(half, d):
        c, dz, dh, dl, dx = digits(d)
        return place_of(
            lax.rem(px + 8 - 2 * dx - half, 4),
            lax.rem(py + dl, 2),
            lax.rem(y_hi + dh, 2),
            lax.rem(z + 4 - dz, 4),
            lax.rem(core + c, 2),
        )

    def send_to(t, src, dst, ssem, rsem):
        return pltpu.make_async_remote_copy(
            src_ref=src,
            dst_ref=dst,
            send_sem=ssem,
            recv_sem=rsem,
            device_id={"pool": lax.div(t, 16), "expert": lax.rem(t, 16)},
            device_id_type=MESH,
        )

    def out_copy(half, d):
        t = target(half, d)
        return send_to(t, obuf.at[t], rbuf.at[me], out_s, out_r.at[half])

    def pick(half, i):
        places, parts = [], []
        for u in range(4):
            t = target(half, i * 4 + u)
            places.append(t)
            parts.append(jnp.where(slot_ref[pl.ds(t, 1), :] == place, 1.0, 0.0).astype(BF16))
        chosen = jnp.concatenate(parts, axis=0)
        picked = jnp.dot(chosen, att_ref[...].reshape(seqs, HD), preferred_element_type=F32)
        return places, picked.astype(BF16)

    places, picked = pick(0, 0)
    rbuf[me] = picked[0:SLOTS]
    for u in range(1, 4):
        obuf[places[u]] = picked[u * SLOTS : (u + 1) * SLOTS]

    def some(half):
        def step(i, carry):
            places, picked = pick(half, i)
            for u in range(4):
                obuf[places[u]] = picked[u * SLOTS : (u + 1) * SLOTS]
            for u in range(4):
                out_copy(half, i * 4 + u - 3).start()
            return carry

        return step

    lax.fori_loop(1, 16, some(0), 0)
    for u in range(61, 64):
        out_copy(0, u).start()
    places, picked = pick(1, 0)
    for u in range(4):
        obuf[places[u]] = picked[u * SLOTS : (u + 1) * SLOTS]
    out_copy(1, 0).start()
    lax.fori_loop(1, 16, some(1), 0)
    for u in range(61, 64):
        out_copy(1, u).start()

    def many(src, dst, ssem, rsem, number):
        return send_to(
            p * 16 + sib, src.at[pl.ds(0, number)], dst.at[pl.ds(0, number)], ssem, rsem
        )

    for gain in gains:
        gain.wait()
    gain_row = jnp.concatenate([gall_ref[f] for f in range(16)], axis=1)

    def back_copy(half, d):
        t = target(half, d)
        return send_to(t, ybuf.at[t], zbuf.at[me], back_s, back_r.at[half * 4 + lax.div(d, 16)])

    def experts_of(half):
        low = lax.rem(px + half, 2) * 2
        many(obuf, rbuf, out_s, out_r.at[half], 63 + half).wait_recv()

        def norm(i, carry):
            q = lax.div(i, 4)
            first = (low + lax.rem(q, 2) + lax.div(q, 2) * 4) * 16
            at = pl.ds(pl.multiple_of(lax.rem(i, 4) * 16, 16), 16)
            x = jnp.concatenate([rbuf[first + f, at, :] for f in range(16)], axis=1).astype(F32)
            inv = lax.rsqrt(jnp.sum(x * x, axis=1, keepdims=True) / (16 * HD) + EPS)
            xs[pl.ds(pl.multiple_of(i * 16, 16), 16), :] = (x * inv * gain_row).astype(BF16)
            return carry

        lax.fori_loop(0, 16, norm, 0)
        if half == 0:
            ffn[0].wait()
            ffn[1].wait()

        def up(i, carry):
            at = pl.ds(pl.multiple_of(i * 256, 256), 256)
            gate = jnp.dot(xs[...], gw[:, at], preferred_element_type=F32)
            upper = jnp.dot(xs[...], uw[:, at], preferred_element_type=F32)
            hid[:, at] = (gate / (1.0 + jnp.exp(-gate)) * upper).astype(BF16)
            return carry

        lax.fori_loop(0, 3, up, 0)
        if half == 0:
            ffn[2].wait()

        def down(tile, carry):
            at = pl.ds(pl.multiple_of(tile * 256, 256), 256)
            y = jnp.dot(hid[...], dw[:, at], preferred_element_type=F32).astype(BF16)
            for q in range(4):
                first = (low + q % 2 + (q // 2) * 4) * 16
                for h in range(2):
                    ybuf[first + tile * 2 + h] = y[
                        q * SLOTS : (q + 1) * SLOTS, h * HD : (h + 1) * HD
                    ]
            return carry

        lax.fori_loop(0, 8, down, 0)

        def send(d, carry):
            back_copy(half, d).start()
            return carry

        lax.fori_loop(1 - half, 64, send, 0)

    experts_of(0)
    experts_of(1)
    zbuf[me] = ybuf[me]

    mixt[...] = jnp.zeros_like(mixt)

    def gather_back(half, k):
        many(ybuf, zbuf, back_s, back_r.at[half * 4 + k], 15 if half + k == 0 else 16).wait_recv()

        def four(c, carry):
            parts, ys = [], []
            for u in range(4):
                t = origin(half, k * 16 + c * 4 + u)
                parts.append(
                    jnp.where(
                        slot_ref[pl.ds(t, 1), :] == place, wt_ref[pl.ds(t, 1), :], 0.0
                    ).astype(BF16)
                )
                ys.append(zbuf[t])
            chosen = jnp.concatenate(parts, axis=0)
            y = jnp.concatenate(ys, axis=0)
            mixt[...] += lax.dot_general(y, chosen, TN, preferred_element_type=F32)
            return carry

        lax.fori_loop(0, 4, four, 0)

    for half in range(2):
        for k in range(4):
            gather_back(half, k)
    mix_ref[...] = mixt[...].T.astype(BF16)
    many(obuf, rbuf, out_s, out_r.at[0], 127).wait_send()
    many(ybuf, zbuf, back_s, back_r.at[0], 127).wait_send()
    for g in range(4):
        own_y(g).wait_send()
        for kind in (0, 2) if g < 2 else range(4):
            z_copy(kind, g, 0).wait_send()
            z_copy(kind, g, 1).wait_send()
        if g < 2:
            for kind in range(4):
                y_more(kind, g).wait_send()
    send_w.wait_send()
    send_res.wait_send()
    send_out.wait_send()


def hand_over(a_ref, b_ref, c_ref, d_ref):
    c_ref[...] = a_ref[...]
    d_ref[...] = b_ref[...]


def shards(
    queries,
    kv_cache,
    block_index,
    lengths,
    residual,
    out_weight,
    norm_gain,
    expert_ids,
    route_weights,
    gate_weight,
    up_weight,
    down_weight,
):
    rows = queries.shape[0]
    span = kv_cache.shape[0] * kv_cache.shape[1]
    width = kv_cache.shape[2]
    wide, hidden = gate_weight.shape[1:]
    dma = pltpu.SemaphoreType.DMA
    att, mixed = pl.pallas_call(
        layer,
        out_shape=(
            jax.ShapeDtypeStruct((8, 2, 32, HD), BF16),
            jax.ShapeDtypeStruct((512, HD), BF16),
        ),
        in_specs=[VM, ANY, VM, VM, VM, ANY, VM, VM, VM, ANY, ANY, ANY],
        out_specs=(VM, VM),
        scratch_shapes=[
            pltpu.VMEM((width // HD, span, HD), BF16),
            pltpu.VMEM(out_weight.shape, BF16),
            pltpu.VMEM(out_weight.shape, BF16),
            pltpu.VMEM((8, 32, HD), BF16),
            pltpu.VMEM((8, 4, 32, 8 * HD), BF16),
            pltpu.VMEM((256, span), F32),
            pltpu.VMEM((256, span), BF16),
            pltpu.VMEM((256, HD), F32),
            pltpu.VMEM((rows, span), F32),
            pltpu.VMEM((8, 32, HD), BF16),
            pltpu.VMEM((2, 256, HD), F32),
            pltpu.VMEM((128, 128), jnp.int32),
            pltpu.VMEM((16, 1, HD), F32),
            pltpu.VMEM((128, 512), F32),
            pltpu.VMEM((128, 512), F32),
            pltpu.VMEM((wide, hidden), BF16),
            pltpu.VMEM((wide, hidden), BF16),
            pltpu.VMEM((hidden, wide), BF16),
            pltpu.VMEM((128, SLOTS, HD), BF16),
            pltpu.VMEM((128, SLOTS, HD), BF16),
            pltpu.VMEM((128, SLOTS, HD), BF16),
            pltpu.VMEM((128, SLOTS, HD), BF16),
            pltpu.VMEM((256, wide), BF16),
            pltpu.VMEM((256, hidden), BF16),
            pltpu.VMEM((HD, 512), F32),
            dma((8,)),
            dma,
            dma((4,)),
            dma((4,)),
            dma((4, 4, 2)),
            dma((4, 4, 2)),
            dma((3,)),
            dma((3,)),
            dma((16,)),
            dma((16,)),
            dma((3,)),
            dma,
            dma((2,)),
            dma,
            dma((8,)),
            dma((4, 2)),
            dma((4, 2)),
        ],
        compiler_params=pltpu.CompilerParams(
            collective_id=0, has_side_effects=True, vmem_limit_bytes=60 * 1024 * 1024
        ),
        name="layer",
    )(
        queries,
        kv_cache.reshape(span, width),
        block_index.T,
        lengths.reshape(1, rows),
        residual.reshape(8, 2, 32, HD),
        out_weight,
        norm_gain.reshape(1, HD),
        expert_ids.T,
        route_weights.T,
        gate_weight,
        up_weight,
        down_weight,
    )
    return pl.pallas_call(
        hand_over,
        out_shape=(
            jax.ShapeDtypeStruct((512, HD), BF16),
            jax.ShapeDtypeStruct((512, HD), BF16),
        ),
        in_specs=[VM, VM],
        out_specs=(VM, VM),
        name="hand_over",
    )(att.reshape(512, HD), mixed)


def solution(mesh):
    return jax.shard_map(
        shards,
        mesh=mesh,
        in_specs=(
            P(("pool", "expert"), None),
            P(("pool", "expert"), None, None),
            P(("pool", "expert"), None),
            P(("pool", "expert")),
            P("pool", "expert"),
            P(None, "expert"),
            P("expert"),
            P("pool", None),
            P("pool", None),
            P(("pool", "expert"), None, None),
            P(("pool", "expert"), None, None),
            P(("pool", "expert"), None, None),
        ),
        out_specs=(P("pool", "expert"), P("pool", "expert")),
        check_vma=False,
    )
```

```python
import math

import jax
import jax.numpy as jnp
from jax import lax
from jax.experimental import pallas as pl
from jax.experimental.pallas import tpu as pltpu
from jax.sharding import PartitionSpec as P

HD = 128
EPS = 1e-06
MESH = pl.DeviceIdType.MESH
F32 = jnp.float32
BF16 = jnp.bfloat16
VM = pl.BlockSpec(memory_space=pltpu.VMEM)
ANY = pl.BlockSpec(memory_space=pl.ANY)
NT = (((1,), (1,)), ((), ()))
TN = (((0,), (0,)), ((), ()))
SLOTS = 64


def layer(
    q_ref,
    kv_hbm,
    bi_ref,
    len_ref,
    res_ref,
    w_hbm,
    gain_ref,
    ids_ref,
    rw_ref,
    g_hbm,
    u_hbm,
    d_hbm,
    att_ref,
    mix_ref,
    kv,
    wown,
    wsib,
    ressib,
    gath,
    s_scr,
    p_scr,
    linv,
    bias,
    stage,
    acc,
    table,
    gall_ref,
    slot_ref,
    wt_ref,
    gw,
    uw,
    dw,
    obuf,
    rbuf,
    ybuf,
    zbuf,
    xs,
    hid,
    mixt,
    in_sem,
    w_sem,
    y_s,
    y_r,
    z_s,
    z_r,
    sib_s,
    sib_r,
    gain_s,
    gain_r,
    ffn_sem,
    out_s,
    out_r,
    back_s,
    back_r,
    ym_s,
    ym_r,
):
    p = lax.axis_index("pool")
    e = lax.axis_index("expert")
    core = e % 2
    chip = e // 2
    y_hi = chip // 4
    z = chip % 4
    sib = e + 1 - 2 * core
    chip_y = chip + 4 - 8 * y_hi
    z_up = (z + 1) % 4
    z_dn = (z + 3) % 4
    z_op = (z + 2) % 4
    chip_up = y_hi * 4 + z_up
    chip_dn = y_hi * 4 + z_dn
    chip_op = y_hi * 4 + z_op
    flip = 4 - 8 * y_hi
    dev_y = chip_y * 2 + core
    dev_up = chip_up * 2 + core
    dev_dn = chip_dn * 2 + core

    me = p * 16 + e
    barrier = pltpu.get_barrier_semaphore()

    def fetch(i):
        return pltpu.make_async_copy(kv_hbm.at[:, pl.ds(i * HD, HD)], kv.at[i], in_sem.at[i])

    fetch_w = pltpu.make_async_copy(w_hbm, wown, w_sem)
    for g in range(4):
        fetch(g).start()
        fetch(4 + g).start()
    ffn = [
        pltpu.make_async_copy(g_hbm.at[0], gw, ffn_sem.at[0]),
        pltpu.make_async_copy(u_hbm.at[0], uw, ffn_sem.at[1]),
        pltpu.make_async_copy(d_hbm.at[0], dw, ffn_sem.at[2]),
    ]

    def greet(d, carry):
        t = lax.rem(me + d, 128)
        pl.semaphore_signal(
            barrier,
            inc=1,
            device_id={"pool": lax.div(t, 16), "expert": lax.rem(t, 16)},
            device_id_type=MESH,
        )
        return carry

    lax.fori_loop(1, 128, greet, 0)

    rows, span = bias.shape
    lane = lax.broadcasted_iota(jnp.int32, (rows, span), 1)
    block = lane // 64
    offset = lane % 64
    count = jnp.zeros((rows, span), F32)
    table[...] = jnp.zeros_like(table)
    table[0:8, 0:rows] = bi_ref[...]
    table[8:16, 0:rows] = jnp.broadcast_to(len_ref[...], (8, rows))
    turned = table[...].T[0:rows, :]
    for j in range(8):
        live = (block == turned[:, j : j + 1]) & (offset < turned[:, 8:9] - 64 * j)
        count = count + jnp.where(live, 1.0, 0.0)
    bias[...] = jnp.where(count > 0.0, jnp.log2(jnp.maximum(count, 1.0)), -1e30)

    factor = HD ** (-0.5) * math.log2(math.e)

    def attend(g):
        fetch(g).wait()
        query = jnp.concatenate(
            [q_ref[:, (g * 8 + i) * HD : (g * 8 + i + 1) * HD] for i in range(8)], axis=0
        )
        s_scr[...] = lax.dot_general(query, kv[g], NT, preferred_element_type=F32)

        def soften(r, carry):
            for v in range(4):
                at = pl.ds(pl.multiple_of(r * 64 + v * 16, 16), 16)
                x = s_scr[at, :] * factor + bias[(v % 2) * 16 : (v % 2) * 16 + 16, :]
                top = jnp.max(x, axis=1, keepdims=True)
                ex = jnp.exp2(x - top)
                total = jnp.sum(ex, axis=1, keepdims=True)
                p_scr[at, :] = ex.astype(BF16)
                linv[at, :] = jnp.broadcast_to(1.0 / total, (16, HD))
            return carry

        lax.fori_loop(0, 4, soften, 0)
        fetch(4 + g).wait()
        o = jnp.dot(p_scr[...], kv[4 + g], preferred_element_type=F32) * linv[...]
        o = o.astype(BF16)
        for i in range(8):
            gath[chip, g, :, i * HD : (i + 1) * HD] = o[i * 32 : (i + 1) * 32]

    def remote(src, dst, ssem, rsem, dev):
        return pltpu.make_async_remote_copy(
            src_ref=src,
            dst_ref=dst,
            send_sem=ssem,
            recv_sem=rsem,
            device_id={"expert": dev},
            device_id_type=MESH,
        )

    lo, hi = pl.ds(0, 16), pl.ds(16, 16)

    def block_copy(c, g, ssem, rsem, dev, part=None):
        ref = gath.at[c, g] if part is None else gath.at[c, g, part]
        return remote(ref, ref, ssem, rsem, dev)

    def own_y(g):
        return block_copy(chip, g, y_s.at[g], y_r.at[g], dev_y)

    def z_copy(kind, g, way):
        dev = dev_up if way == 0 else dev_dn
        ss, rs = z_s.at[kind, g, way], z_r.at[kind, g, way]
        if kind == 0:
            return block_copy(chip, g, ss, rs, dev)
        if kind == 1:
            return block_copy(chip_y, g, ss, rs, dev)
        source = chip_dn if way == 0 else chip_up
        if kind == 3:
            source = source + flip
        return block_copy(source, g, ss, rs, dev, lo if way == 0 else hi)

    def send_own(g):
        z_copy(0, g, 0).start()
        z_copy(0, g, 1).start()
        own_y(g).start()

    def send_partner(g):
        own_y(g).wait_recv()
        z_copy(1, g, 0).start()
        z_copy(1, g, 1).start()

    def relay(kind, g):
        for way in (0, 1):
            z_copy(kind, g, way).wait_recv()
            z_copy(kind + 2, g, way).start()

    def finish(g):
        for way in (0, 1):
            z_copy(2, g, way).wait_recv()
            z_copy(3, g, way).wait_recv()

    def y_more(kind, g):
        ss, rs = ym_s.at[kind, g], ym_r.at[kind, g]
        if kind < 2:
            return block_copy(chip_up if kind else chip_dn, g, ss, rs, dev_y)
        return block_copy(chip_op, g, ss, rs, dev_y, hi if kind == 3 else lo)

    def first_z(g):
        for way in (0, 1):
            z_copy(0, g, way).wait_recv()
            z_copy(2, g, way).start()
            y_more(way, g).start()

    def second_z(g):
        for way in (0, 1):
            z_copy(2, g, way).wait_recv()
            y_more(2 + way, g).start()

    def finish_y(g):
        own_y(g).wait_recv()
        for kind in range(4):
            y_more(kind, g).wait_recv()

    def project(g):
        depth = 8 * HD
        at = pl.ds(g * depth, depth)
        rows_g = gath[:, g].reshape(256, depth)
        part = jnp.dot(rows_g, wown[at, :], preferred_element_type=F32)
        other = jnp.dot(rows_g, wsib[at, :], preferred_element_type=F32)
        if g == 0:
            acc[0] = part
            acc[1] = other
        else:
            acc[0] += part
            acc[1] += other

    attend(0)
    fetch_w.start()
    pl.semaphore_wait(barrier, 127)
    send_own(0)
    send_w = remote(w_hbm, wsib, sib_s.at[0], sib_r.at[0], sib)
    send_w.start()
    send_res = remote(res_ref.at[:, 1 - core], ressib, sib_s.at[1], sib_r.at[1], sib)
    send_res.start()
    gall_ref[e] = gain_ref[...]
    gains = [
        remote(gain_ref, gall_ref.at[e], gain_s.at[d], gain_r.at[d], (e + d) % 16)
        for d in range(1, 16)
    ]
    for gain in gains:
        gain.start()
    attend(1)
    for copy in ffn:
        copy.start()
    send_own(1)
    attend(2)
    send_own(2)
    first_z(0)
    attend(3)
    send_own(3)
    first_z(1)
    second_z(0)
    send_partner(2)
    experts, seqs = slot_ref.shape
    which = lax.broadcasted_iota(jnp.int32, (experts, seqs), 0)
    named = jnp.zeros((experts, seqs), F32)
    weight = jnp.zeros((experts, seqs), F32)
    for k in range(8):
        same = which == ids_ref[k : k + 1, :]
        named = named + jnp.where(same, 1.0, 0.0)
        weight = weight + jnp.where(same, rw_ref[k : k + 1, :], 0.0)
    wt_ref[...] = weight
    early = lax.broadcasted_iota(jnp.int32, (seqs, seqs), 0)
    late = lax.broadcasted_iota(jnp.int32, (seqs, seqs), 1)
    ahead = jnp.where(early < late, 1.0, 0.0).astype(BF16)
    slots = jnp.dot(named.astype(BF16), ahead, preferred_element_type=F32)
    slot_ref[...] = jnp.where(named > 0.0, slots, -1.0)
    relay(0, 2)
    second_z(1)
    send_partner(3)
    fetch_w.wait()
    send_w.wait_recv()
    relay(0, 3)
    relay(1, 2)
    finish_y(0)
    project(0)
    relay(1, 3)
    finish_y(1)
    project(1)
    finish(2)
    project(2)
    finish(3)
    project(3)
    send_res.wait_recv()
    stage[...] = (ressib[...].astype(F32) + acc[1].reshape(8, 32, HD)).astype(BF16)
    send_out = remote(stage, att_ref.at[:, core], sib_s.at[2], sib_r.at[2], sib)
    send_out.start()
    att_ref[:, core] = (res_ref[:, core].astype(F32) + acc[0].reshape(8, 32, HD)).astype(BF16)
    send_out.wait_recv()

    place = lax.broadcasted_iota(jnp.int32, (SLOTS, seqs), 0).astype(F32)
    px, py = p // 2, p % 2

    def place_of(xx, yl, yh, zz, c):
        return (xx * 2 + yl) * 16 + yh * 8 + zz * 2 + c

    def digits(d):
        d = lax.rem(d * 13, 32)
        c = lax.rem(d, 2)
        d = lax.div(d, 2)
        dz = lax.rem(d, 4)
        d = lax.div(d, 4)
        return c, dz, lax.rem(d, 2), lax.div(d, 2)

    def there(q, w, way):
        return lax.rem(px + 8 + way * q + 2 * w, 4), lax.rem(py + w, 2)

    def target(q, d, way=1):
        c, dz, dh, w = digits(d)
        xx, yl = there(q, w, way)
        return place_of(
            xx, yl, lax.rem(y_hi + dh, 2), lax.rem(z + dz, 4), lax.rem(core + c, 2)
        )

    def origin(q, d):
        c, dz, dh, w = digits(d)
        xx, yl = there(q, w, 1)
        return place_of(
            xx, yl, lax.rem(y_hi + dh, 2), lax.rem(z + 4 - dz, 4), lax.rem(core + c, 2)
        )

    def send_to(t, src, dst, ssem, rsem):
        return pltpu.make_async_remote_copy(
            src_ref=src,
            dst_ref=dst,
            send_sem=ssem,
            recv_sem=rsem,
            device_id={"pool": lax.div(t, 16), "expert": lax.rem(t, 16)},
            device_id_type=MESH,
        )

    def out_copy(quarter, d):
        t = target(quarter, d)
        return send_to(t, obuf.at[t], rbuf.at[me], out_s, out_r.at[quarter])

    def pick(quarter, i):
        places, parts = [], []
        for u in range(4):
            t = target(quarter, i * 4 + u)
            places.append(t)
            parts.append(jnp.where(slot_ref[pl.ds(t, 1), :] == place, 1.0, 0.0).astype(BF16))
        chosen = jnp.concatenate(parts, axis=0)
        picked = jnp.dot(chosen, att_ref[...].reshape(seqs, HD), preferred_element_type=F32)
        return places, picked.astype(BF16)

    places, picked = pick(0, 0)
    rbuf[me] = picked[0:SLOTS]
    for u in range(1, 4):
        obuf[places[u]] = picked[u * SLOTS : (u + 1) * SLOTS]

    def some(quarter):
        def step(i, carry):
            places, picked = pick(quarter, i)
            for u in range(4):
                obuf[places[u]] = picked[u * SLOTS : (u + 1) * SLOTS]
            for u in range(4):
                out_copy(quarter, i * 4 + u - 3).start()
            return carry

        return step

    lax.fori_loop(1, 8, some(0), 0)
    for u in range(29, 32):
        out_copy(0, u).start()
    for q in range(1, 4):
        places, picked = pick(q, 0)
        for u in range(4):
            obuf[places[u]] = picked[u * SLOTS : (u + 1) * SLOTS]
        out_copy(q, 0).start()
        lax.fori_loop(1, 8, some(q), 0)
        for u in range(29, 32):
            out_copy(q, u).start()

    def many(src, dst, ssem, rsem, number):
        return send_to(
            p * 16 + sib, src.at[pl.ds(0, number)], dst.at[pl.ds(0, number)], ssem, rsem
        )

    for gain in gains:
        gain.wait()
    gain_row = jnp.concatenate([gall_ref[f] for f in range(16)], axis=1)

    def back_copy(quarter, d):
        t = target(quarter, d, -1)
        return send_to(t, ybuf.at[t], zbuf.at[me], back_s, back_r.at[quarter * 2 + lax.div(d, 16)])

    def experts_of(quarter):
        many(obuf, rbuf, out_s, out_r.at[quarter], 32 if quarter else 31).wait_recv()

        def pool_of(w):
            xx, yl = there(quarter, w, -1)
            return (xx * 2 + yl) * 16

        def norm(i, carry):
            first = pool_of(lax.div(i, 4))
            at = pl.ds(pl.multiple_of(lax.rem(i, 4) * 16, 16), 16)
            x = jnp.concatenate([rbuf[first + f, at, :] for f in range(16)], axis=1).astype(F32)
            inv = lax.rsqrt(jnp.sum(x * x, axis=1, keepdims=True) / (16 * HD) + EPS)
            xs[pl.ds(pl.multiple_of(i * 16, 16), 16), :] = (x * inv * gain_row).astype(BF16)
            return carry

        lax.fori_loop(0, 8, norm, 0)
        if quarter == 0:
            ffn[0].wait()
            ffn[1].wait()

        def up(i, carry):
            at = pl.ds(pl.multiple_of(i * 256, 256), 256)
            gate = jnp.dot(xs[...], gw[:, at], preferred_element_type=F32)
            upper = jnp.dot(xs[...], uw[:, at], preferred_element_type=F32)
            hid[:, at] = (gate / (1.0 + jnp.exp(-gate)) * upper).astype(BF16)
            return carry

        lax.fori_loop(0, 3, up, 0)
        if quarter == 0:
            ffn[2].wait()

        def down(tile, carry):
            at = pl.ds(pl.multiple_of(tile * 256, 256), 256)
            y = jnp.dot(hid[...], dw[:, at], preferred_element_type=F32).astype(BF16)
            for q in range(2):
                first = pool_of(q)
                for h in range(2):
                    ybuf[first + tile * 2 + h] = y[
                        q * SLOTS : (q + 1) * SLOTS, h * HD : (h + 1) * HD
                    ]
            return carry

        lax.fori_loop(0, 8, down, 0)

        def send(d, carry):
            back_copy(quarter, d).start()
            return carry

        lax.fori_loop(0 if quarter else 1, 32, send, 0)

    for q in range(4):
        experts_of(q)
    zbuf[me] = ybuf[me]

    mixt[...] = jnp.zeros_like(mixt)

    def gather_back(quarter, k):
        many(ybuf, zbuf, back_s, back_r.at[quarter * 2 + k], 15 if quarter + k == 0 else 16).wait_recv()

        def four(c, carry):
            parts, ys = [], []
            for u in range(4):
                t = origin(quarter, k * 16 + c * 4 + u)
                parts.append(
                    jnp.where(
                        slot_ref[pl.ds(t, 1), :] == place, wt_ref[pl.ds(t, 1), :], 0.0
                    ).astype(BF16)
                )
                ys.append(zbuf[t])
            chosen = jnp.concatenate(parts, axis=0)
            y = jnp.concatenate(ys, axis=0)
            mixt[...] += lax.dot_general(y, chosen, TN, preferred_element_type=F32)
            return carry

        lax.fori_loop(0, 4, four, 0)

    for quarter in range(4):
        for k in range(2):
            gather_back(quarter, k)
    mix_ref[...] = mixt[...].T.astype(BF16)
    many(obuf, rbuf, out_s, out_r.at[0], 127).wait_send()
    many(ybuf, zbuf, back_s, back_r.at[0], 127).wait_send()
    for g in range(4):
        own_y(g).wait_send()
        for kind in (0, 2) if g < 2 else range(4):
            z_copy(kind, g, 0).wait_send()
            z_copy(kind, g, 1).wait_send()
        if g < 2:
            for kind in range(4):
                y_more(kind, g).wait_send()
    send_w.wait_send()
    send_res.wait_send()
    send_out.wait_send()


def hand_over(a_ref, b_ref, c_ref, d_ref):
    c_ref[...] = a_ref[...]
    d_ref[...] = b_ref[...]


def shards(
    queries,
    kv_cache,
    block_index,
    lengths,
    residual,
    out_weight,
    norm_gain,
    expert_ids,
    route_weights,
    gate_weight,
    up_weight,
    down_weight,
):
    rows = queries.shape[0]
    span = kv_cache.shape[0] * kv_cache.shape[1]
    width = kv_cache.shape[2]
    wide, hidden = gate_weight.shape[1:]
    dma = pltpu.SemaphoreType.DMA
    att, mixed = pl.pallas_call(
        layer,
        out_shape=(
            jax.ShapeDtypeStruct((8, 2, 32, HD), BF16),
            jax.ShapeDtypeStruct((512, HD), BF16),
        ),
        in_specs=[VM, ANY, VM, VM, VM, ANY, VM, VM, VM, ANY, ANY, ANY],
        out_specs=(VM, VM),
        scratch_shapes=[
            pltpu.VMEM((width // HD, span, HD), BF16),
            pltpu.VMEM(out_weight.shape, BF16),
            pltpu.VMEM(out_weight.shape, BF16),
            pltpu.VMEM((8, 32, HD), BF16),
            pltpu.VMEM((8, 4, 32, 8 * HD), BF16),
            pltpu.VMEM((256, span), F32),
            pltpu.VMEM((256, span), BF16),
            pltpu.VMEM((256, HD), F32),
            pltpu.VMEM((rows, span), F32),
            pltpu.VMEM((8, 32, HD), BF16),
            pltpu.VMEM((2, 256, HD), F32),
            pltpu.VMEM((128, 128), jnp.int32),
            pltpu.VMEM((16, 1, HD), F32),
            pltpu.VMEM((128, 512), F32),
            pltpu.VMEM((128, 512), F32),
            pltpu.VMEM((wide, hidden), BF16),
            pltpu.VMEM((wide, hidden), BF16),
            pltpu.VMEM((hidden, wide), BF16),
            pltpu.VMEM((128, SLOTS, HD), BF16),
            pltpu.VMEM((128, SLOTS, HD), BF16),
            pltpu.VMEM((128, SLOTS, HD), BF16),
            pltpu.VMEM((128, SLOTS, HD), BF16),
            pltpu.VMEM((128, wide), BF16),
            pltpu.VMEM((128, hidden), BF16),
            pltpu.VMEM((HD, 512), F32),
            dma((8,)),
            dma,
            dma((4,)),
            dma((4,)),
            dma((4, 4, 2)),
            dma((4, 4, 2)),
            dma((3,)),
            dma((3,)),
            dma((16,)),
            dma((16,)),
            dma((3,)),
            dma,
            dma((4,)),
            dma,
            dma((8,)),
            dma((4, 2)),
            dma((4, 2)),
        ],
        compiler_params=pltpu.CompilerParams(
            collective_id=0, has_side_effects=True, vmem_limit_bytes=60 * 1024 * 1024
        ),
        name="layer",
    )(
        queries,
        kv_cache.reshape(span, width),
        block_index.T,
        lengths.reshape(1, rows),
        residual.reshape(8, 2, 32, HD),
        out_weight,
        norm_gain.reshape(1, HD),
        expert_ids.T,
        route_weights.T,
        gate_weight,
        up_weight,
        down_weight,
    )
    return pl.pallas_call(
        hand_over,
        out_shape=(
            jax.ShapeDtypeStruct((512, HD), BF16),
            jax.ShapeDtypeStruct((512, HD), BF16),
        ),
        in_specs=[VM, VM],
        out_specs=(VM, VM),
        name="hand_over",
    )(att.reshape(512, HD), mixed)


def solution(mesh):
    return jax.shard_map(
        shards,
        mesh=mesh,
        in_specs=(
            P(("pool", "expert"), None),
            P(("pool", "expert"), None, None),
            P(("pool", "expert"), None),
            P(("pool", "expert")),
            P("pool", "expert"),
            P(None, "expert"),
            P("expert"),
            P("pool", None),
            P("pool", None),
            P(("pool", "expert"), None, None),
            P(("pool", "expert"), None, None),
            P(("pool", "expert"), None, None),
        ),
        out_specs=(P("pool", "expert"), P("pool", "expert")),
        check_vma=False,
    )
```
